32 devices in a mesh: parts: 2 (over y), db: 4 (over z), blk: 4 (over x, core).
Axes of the slice: x: 2, y: 2, z: 4, core: 2. Of those that a mesh axis runs over, the one named last changes fastest.
Arguments:
- queries: bfloat16 [8192, 768], P(('parts', 'db', 'blk')), parts along dimension 0, may hold values from -6 to 6
- projection: bfloat16 [768, 768], replicated, may hold values from -0.21875 to 0.21875
- vectors: bfloat16 [768, 32768], P(None, ('parts', 'db', 'blk')), parts along dimension 1, may hold values from -0.21875 to 0.21875
- bins: int32 [32768], P(('parts', 'db', 'blk')), parts along dimension 0, may hold values from 0 to 127, as said below
- routes: int32 [8192, 1], P(('parts', 'db', 'blk')), parts along dimension 0, may hold values from 0 to 3; in each aligned block of 256 rows (0 to 255, 256 to 511, ...) at most 128 rows name the same one
Outputs:
- best: float32 [8192, 128], P(('parts', 'db', 'blk')), parts along dimension 0
The draws below stay inside these ranges and needn't reach their ends.
There are 2 independent parts, one for each index of `parts`. The reference program is written for one: setup_inputs(seed, part) draws one part's arguments, and reference() takes and returns one part's arrays. A program takes and returns all parts, laid end to end along the dimension named above; an argument that names none is the same for every part. Nothing has to cross between parts.
Inputs may be any that keep to these rules, and one draw needn't show every extreme that they name: Within every aligned block of 1024 entries each of the 128 bins occurs exactly 1024 // 128 times. `routes`: within every aligned block of 256 rows no group is named by more than 128 rows; in every draw some block names some group exactly 128 times.
All inputs are finite; a program needn't handle non-finite values.
Results may differ from the reference program's by a relative error of at most 0.0014.
Values may be sent and summed in bfloat16 or wider, within the bound.
A program may use at most 64 MiB of HBM per device.

```python
import math
import jax
import jax.numpy as jnp
import numpy as np
from jax import lax

D = 768
BINS = 128
REQ_DEV = 256
VEC_DEV = 1024
CAP = 128
REQUESTS = 4096
VECTORS = 16384
N_DB = 4
N_BLK = 4


def draw_bins(key, part):
    blocks_total = VECTORS // VEC_DEV
    block_keys = jax.random.split(jax.random.fold_in(key, 7), blocks_total)
    pattern = jnp.arange(VEC_DEV, dtype=jnp.int32) % BINS

    def shuffle_block(block_key):
        return jax.random.permutation(block_key, pattern)
    return jax.vmap(shuffle_block)(block_keys).reshape(-1)


def level_of(key, dims, shards, smallest, high):
    def one(dim, shards_of):
        steps = jax.random.uniform(jax.random.fold_in(jax.random.fold_in(key, 6), dim), (shards_of,), jnp.float32, smallest / len(shards), high / len(shards))
        return jnp.repeat(jnp.exp(steps), dims[dim] // shards_of).reshape((-1,) + (1,) * (len(dims) - dim - 1))

    level = one(*shards[0])
    for cut in shards[1:]:
        level = level * one(*cut)
    return level


def assign_block(stream_key, own, number, rows, count, top, limit, slope):
    order = jax.random.permutation(stream_key, count)
    packed, usual = portions_of(count, rows * top, limit, slope, True), portions_of(count, rows * top, limit, slope, False)
    places = jnp.arange(count)

    def named(sizes, offset_by):
        used = int((sizes > 0).sum())
        fixed = max(1, used // 4)
        shifted = fixed + (places - fixed + offset_by * (used - fixed)) % max(1, count - fixed)
        return jnp.zeros((count,), jnp.int32).at[order[jnp.where(places < fixed, places, shifted)]].set(jnp.asarray(sizes, jnp.int32))

    sizes = jnp.where(number % 4 == 0, named(packed, number // 4), named(usual, number - number // 4 - 1))
    mixed = jax.random.permutation(jax.random.fold_in(own, 3), count)
    source_of, receiver = mixed[0:count // 2 * 2:2], mixed[1:count // 2 * 2:2]
    margin = jnp.minimum(sizes[source_of] - 1, limit - sizes[receiver]) // 2
    margin = jnp.where((source_of == order[0]) | (receiver == order[0]) | (sizes[receiver] == 0), 0, jnp.maximum(margin, 0))
    shifted = jax.random.randint(jax.random.fold_in(own, 4), (count // 2,), 0, 1 << 20) % (margin + 1)
    sizes = sizes.at[source_of].add(-shifted).at[receiver].add(shifted)
    items = jnp.searchsorted(jnp.cumsum(sizes), jnp.arange(rows * top), side="right").astype(jnp.int32)
    table = items.reshape(top, rows).T
    table = table[jax.random.permutation(jax.random.fold_in(own, 1), rows)]
    offset_by = jax.random.randint(jax.random.fold_in(own, 2), (rows, 1), 0, top)
    return jnp.take_along_axis(table, (jnp.arange(top)[None, :] + offset_by) % top, axis=1)


def portions_of(count, total, bound, skew, full):
    portions = [(1 << 20) // math.isqrt(grade ** skew) + 1 for grade in range(1, count + 1)]
    largest = bound if full else min(bound, max(-(-total // count), total * portions[0] // sum(portions)))
    least = 1 if total - largest >= count - 1 else 0
    holding, rest = [largest] + [least] * (count - 1), total - largest - least * (count - 1)
    while rest > 0:
        movable = [i for i in range(1, count) if holding[i] < largest] or [i for i in range(1, count) if holding[i] < bound]
        mass, left = sum([portions[i] for i in movable]), rest
        for i in movable:
            addition = min(bound - holding[i], max(1, left * portions[i] // mass), rest)
            holding[i] = holding[i] + addition
            rest = rest - addition
    return np.array(holding)


def scatter_about(own_key, shape, scale, limit, shards=(), kind=jnp.bfloat16):
    drawn = scale * jax.random.normal(own_key, shape, jnp.float32)
    if shards:
        drawn = drawn * level_of(own_key, shape, shards, -0.22, 0.18)
    return jnp.clip(drawn, -limit, limit).astype(kind)


def setup_inputs(seed: int = 0, part: int = 0) -> dict:
    streams_of = jax.random.split(jax.random.key(seed), 6)
    part_keys = jax.random.split(jax.random.fold_in(streams_of[5], part), 6)
    queries = scatter_about(part_keys[0], (REQUESTS, D), 1.0, 6.0, ((0, 16),))
    projection = scatter_about(streams_of[1], (D, D), D ** -0.5, 0.21875)
    vectors = scatter_about(part_keys[2], (D, VECTORS), (D ** -0.5), 0.21875, ((1, 16),))
    bins = draw_bins(jax.random.fold_in(jax.random.fold_in(streams_of[5], part), 71), part)
    routes_keys = jax.random.split(jax.random.fold_in(part_keys[4], 1), REQUESTS // REQ_DEV)
    routes_turns = jax.random.permutation(jax.random.fold_in(part_keys[4], 3), REQUESTS // REQ_DEV)
    routes = jax.vmap(lambda own, number: assign_block(jax.random.fold_in(part_keys[4], 2), own, number, REQ_DEV, N_DB, 1, CAP, 2))(routes_keys, routes_turns).reshape((REQUESTS, 1))
    return {"queries": queries, "projection": projection, "vectors": vectors, "bins": bins, "routes": routes}


logit_scale = 10.0

def reference(queries, projection, vectors, bins, routes):
    devices_all = N_DB * N_BLK
    capacity = 2 * REQ_DEV // N_DB
    per_bin = VEC_DEV // BINS
    projected = jnp.dot(queries, projection, preferred_element_type=jnp.float32)
    normed = (projected * lax.rsqrt(lax.optimization_barrier(jnp.sum(projected * projected, axis=1, keepdims=True)) + 1e-06)).astype(jnp.bfloat16)
    target = routes[:, 0].reshape(devices_all, REQ_DEV)
    one_hot = (target[:, :, None] == jnp.arange(N_DB, dtype=jnp.int32)[None, None, :]).astype(jnp.int32)
    slot_index = lax.optimization_barrier(jnp.sum((jnp.cumsum(one_hot, axis=1) - one_hot) * one_hot, axis=2))
    requester = jnp.arange(devices_all, dtype=jnp.int32)[:, None]
    position = (target * (devices_all * capacity) + requester * capacity + slot_index).reshape(-1).astype(jnp.int32)
    dispatched = jnp.zeros((N_DB * devices_all * capacity, D), jnp.float32).at[position].set(normed.astype(jnp.float32))
    dispatched = dispatched.reshape(N_DB, devices_all * capacity, D)
    slab_all = vectors.reshape(D, devices_all, VEC_DEV)
    ordering = jnp.argsort(bins.reshape(devices_all, VEC_DEV), axis=1, stable=True).astype(jnp.int32)
    ordering = ordering.reshape(devices_all, BINS, per_bin).transpose(0, 2, 1).reshape(devices_all, VEC_DEV)
    sorted_all = jnp.take_along_axis(slab_all, ordering[None, :, :], axis=2)
    sorted_all = sorted_all.reshape(D, N_DB, N_BLK * VEC_DEV).transpose(1, 0, 2)

    def group_max(operands):
        query_rows, group_slab = operands
        scores = jnp.dot(query_rows, group_slab.astype(jnp.float32), preferred_element_type=jnp.float32)
        return logit_scale * lax.optimization_barrier(jnp.max(scores.reshape(query_rows.shape[0], N_BLK * per_bin, BINS), axis=1))
    maxima = lax.map(group_max, (dispatched, sorted_all))
    return maxima.reshape(-1, BINS)[position]
```

```python
import functools

import jax
import jax.numpy as jnp
from jax import lax
from jax.experimental import pallas as pl
from jax.experimental.pallas import tpu as pltpu
from jax.sharding import PartitionSpec as P

BINS = 128
TILE = 256
logit_scale = 10.0
MESH = pl.DeviceIdType.MESH


CODE_SCALE = 2.0 ** 26


def encode(score):
    scaled = score * CODE_SCALE
    square = scaled * scaled
    fourth = square * square
    return jnp.where(score < 0, -fourth, fourth)


def decode(code):
    root = jnp.sqrt(jnp.sqrt(jnp.abs(code))) * (1.0 / CODE_SCALE)
    return jnp.where(code < 0, -root, root)


def kernel(
    G, NB, cap, sizes,
    q_hbm, p_hbm, v_hbm, b_hbm, r_hbm,
    out_ref,
    q_ref, p_ref, raw, bins_ref, routes_ref, slab, chooser, outgoing, rows, own, xout, xin, back, ans,
    load_sem, z_rs, x_rs, s_rs, xb_rs, zb_rs, sent,
):
    H = NB // 2
    C = len(sizes)
    n, depth = q_ref.shape
    width = raw.shape[1]
    tiles = width // TILE
    f32, bf16 = jnp.float32, jnp.bfloat16
    d = lax.axis_index("db")
    k = lax.axis_index("blk")

    load_r = pltpu.make_async_copy(r_hbm, routes_ref, load_sem.at[0])
    load_q = pltpu.make_async_copy(q_hbm, q_ref, load_sem.at[1])
    load_p = pltpu.make_async_copy(p_hbm, p_ref, load_sem.at[2])
    load_b = pltpu.make_async_copy(b_hbm, bins_ref, load_sem.at[3])
    load_v = pltpu.make_async_copy(v_hbm, raw, load_sem.at[4])

    barrier = pltpu.get_barrier_semaphore()
    for o in range(G - 1, 0, -1):
        pl.semaphore_signal(barrier, inc=1, device_id={"db": d ^ o}, device_id_type=MESH)
    for h in range(1, H):
        pl.semaphore_signal(barrier, inc=1, device_id={"blk": k ^ (2 * h)}, device_id_type=MESH)
    pl.semaphore_signal(barrier, inc=1, device_id={"blk": k ^ 1}, device_id_type=MESH)
    for load in (load_r, load_q, load_p, load_b):
        load.start()

    if G == 4 and C == 4:
        inner = ((d + 1) // 2) % 2
        outer_order = [(2, 0), (2, 1), (2, 2), *((1, c) for c in range(C)), *((3, c) for c in range(C)), (2, 3)]
        inner_order = [(o, c) for o in (1, 2, 3) for c in range(C)]

        def either(a, b):
            return a if a == b else a + inner * (b - a)

        order = [(either(a, i), either(b, j)) for (a, b), (i, j) in zip(outer_order, inner_order)]
        units = [[(0, c) for c in range(C)], order[:4], order[4:8], order[8:10], order[10:]]
    else:
        units = [[(o, c) for o in range(G) for c in range(C)]]
    rank = sizes[0]

    def fixed(start, multiple=16):
        return start if isinstance(start, int) else pl.multiple_of(start, multiple)

    def slots(o, c):
        return pl.ds(fixed(o * cap + c * rank), rank)

    def group(o):
        return pl.ds(fixed(o * cap), cap)

    def block(o, c, h=0, many=1):
        return pl.ds(fixed(o * (H * cap) + (c * H + h) * rank), many * rank)

    def span(u):
        return pl.ds(sum(len(v) for v in units[:u]) * rank, len(units[u]) * rank)

    def z_copy(o, c):
        return pltpu.make_async_remote_copy(
            src_ref=outgoing.at[slots(o, c)], dst_ref=rows.at[block(o, c)],
            send_sem=sent.at[0], recv_sem=z_rs.at[c, o - 1],
            device_id={"db": d ^ o}, device_id_type=MESH)

    def x_copy(u, o, c, h, step):
        return pltpu.make_async_remote_copy(
            src_ref=rows.at[block(o, c, h)], dst_ref=rows.at[block(o, c, h + step)],
            send_sem=sent.at[1], recv_sem=x_rs.at[u, h + step - 1],
            device_id={"blk": k ^ (2 * step)}, device_id_type=MESH)

    def s_copy(t):
        return pltpu.make_async_remote_copy(
            src_ref=slab.at[0, t], dst_ref=slab.at[1, t],
            send_sem=sent.at[2], recv_sem=s_rs.at[t],
            device_id={"blk": k ^ 1}, device_id_type=MESH)

    def xb_copy(u, h):
        return pltpu.make_async_remote_copy(
            src_ref=xout.at[h - 1, span(u)], dst_ref=xin.at[h - 1, span(u)],
            send_sem=sent.at[3], recv_sem=xb_rs.at[u, h - 1],
            device_id={"blk": k ^ (2 * h)}, device_id_type=MESH)

    def zb_copy(o, c):
        return pltpu.make_async_remote_copy(
            src_ref=back.at[slots(o, c)], dst_ref=ans.at[slots(o, c)],
            send_sem=sent.at[4], recv_sem=zb_rs.at[o - 1],
            device_id={"db": d ^ o}, device_id_type=MESH)

    def await_bytes(ref, sem):
        pltpu.make_async_copy(ref, ref, sem).wait()

    def local(o):
        return isinstance(o, int) and o == 0

    load_r.wait()
    target = routes_ref[...]
    pad = max(8, G)
    hot = jnp.where(lax.broadcasted_iota(jnp.int32, (pad, n), 0) == target, 1.0, 0.0)
    before = jnp.where(
        lax.broadcasted_iota(jnp.int32, (n, n), 0) < lax.broadcasted_iota(jnp.int32, (n, n), 1),
        1.0, 0.0).astype(bf16)
    earlier = jnp.dot(hot.astype(bf16), before, preferred_element_type=f32)
    slot = jnp.sum(hot * earlier, axis=0, keepdims=True).astype(jnp.int32)
    position = (target ^ d) * cap + slot

    load_q.wait()
    load_v.start()
    load_p.wait()
    projected = jnp.dot(q_ref[...], p_ref[...], preferred_element_type=f32)
    normed = (
        projected * lax.rsqrt(jnp.sum(projected * projected, axis=1, keepdims=True) + 1e-06)
    ).astype(bf16)

    pl.semaphore_wait(barrier, G - 1 + H)

    def choose(o):
        pick = jnp.where(
            lax.broadcasted_iota(jnp.int32, (cap, n), 0) + o * cap == position, 1.0, 0.0
        ).astype(bf16)
        chooser[group(o), :] = pick
        chosen = jnp.dot(pick, normed, preferred_element_type=f32).astype(bf16)
        if o:
            outgoing[group(o), :] = chosen
            for c in range(C):
                z_copy(o, c).start()
        else:
            for c in range(C):
                rows[block(0, c)] = chosen[c * rank:(c + 1) * rank]
                if H > 1:
                    x_copy(0, 0, c, 0, 1).start()

    for o in [1, 2, 0, *range(3, G)] if G > 2 else range(G):
        choose(o)

    def relay(u, i):
        o, c = units[u][i]
        z_copy(o, c).wait_recv()
        if H > 1:
            x_copy(u, o, c, 0, 1).start()

    load_b.wait()
    load_v.wait()
    bins = bins_ref[...]
    inner_mask = jnp.where(
        lax.broadcasted_iota(jnp.int32, (BINS, BINS), 0)
        < lax.broadcasted_iota(jnp.int32, (BINS, BINS), 1), 1.0, 0.0).astype(bf16)
    run = jnp.zeros((BINS, 1), f32)
    places = []
    for s in range(width // BINS):
        mine = bins[:, s * BINS:(s + 1) * BINS]
        hot = jnp.where(lax.broadcasted_iota(jnp.int32, (BINS, BINS), 0) == mine, 1.0, 0.0)
        earlier = jnp.dot(hot.astype(bf16), inner_mask, preferred_element_type=f32) + run
        turn = jnp.sum(hot * earlier, axis=0, keepdims=True).astype(jnp.int32)
        places.append(turn * BINS + mine)
        run = run + jnp.sum(hot, axis=1, keepdims=True)
    place = jnp.concatenate(places, axis=1)
    for t in range(tiles):
        move = jnp.where(
            lax.broadcasted_iota(jnp.int32, (TILE, width), 0) + t * TILE == place, 1.0, 0.0
        ).astype(bf16)
        slab[0, t] = lax.dot_general(
            raw[...], move, (((1,), (1,)), ((), ())), preferred_element_type=f32).astype(bf16)
        s_copy(t).start()

    def whole(u):
        return rows.at[pl.ds(0, len(units[u]) * rank)]

    def spread(u):
        step = 2
        while step < H:
            for h in range(step):
                if h >= step // 2:
                    await_bytes(whole(u), x_rs.at[u, h - 1])
                for o, c in units[u]:
                    x_copy(u, o, c, h, step).start()
            step *= 2

    met = [False]

    def score(u):
        spread(u)
        for h in range(max(1, H // 2), H):
            await_bytes(whole(u), x_rs.at[u, h - 1])
        first = not met[0]
        met[0] = True
        x = jnp.concatenate([rows[block(o, c, 0, H)] for o, c in units[u]], axis=0)
        best = None
        for side in range(2):
            for t in range(tiles):
                if first and side == 1:
                    s_copy(t).wait_recv()
                sc = jnp.dot(x, slab[side, t], preferred_element_type=f32)
                top = jnp.maximum(sc[:, :BINS], sc[:, BINS:])
                best = top if best is None else jnp.maximum(best, top)
        best = encode(best).astype(bf16)
        to = sum(len(v) for v in units[:u]) * rank
        for i in range(len(units[u])):
            for h in range(H):
                piece = best[(i * H + h) * rank:(i * H + h + 1) * rank]
                if h == 0:
                    own[pl.ds(to + i * rank, rank)] = piece
                else:
                    xout[h - 1, pl.ds(to + i * rank, rank)] = piece
        for h in range(1, H):
            xb_copy(u, h).start()

    def combine(u):
        total = own[span(u)]
        for h in range(1, H):
            xb_copy(u, h).wait_recv()
            total = jnp.maximum(total, xin[h - 1, span(u)])
        for i, (o, c) in enumerate(units[u]):
            piece = total[i * rank:(i + 1) * rank]
            if isinstance(o, int) and o == 0:
                ans[slots(0, c)] = piece
            else:
                back[slots(o, c)] = piece
                zb_copy(o, c).start()

    def unpick(o):
        if o:
            await_bytes(ans.at[group(o)], zb_rs.at[o - 1])
        return lax.dot_general(
            chooser[group(o), :], ans[group(o)], (((0,), (0,)), ((), ())), preferred_element_type=f32)

    if len(units) > 1:
        for i in range(4):
            relay(1, i)
        relay(2, 0)
        relay(2, 1)
        score(0)
        relay(2, 2)
        relay(2, 3)
        score(1)
        combine(0)
        relay(3, 0)
        relay(3, 1)
        relay(4, 0)
        relay(4, 1)
        combine(1)
        score(2)
        score(3)
        combine(2)
        score(4)
        combine(3)
        combine(4)
    else:
        for i, (o, c) in enumerate(units[0]):
            if o:
                relay(0, i)
        score(0)
        combine(0)
    total = unpick(0)
    for o in range(1, G):
        total = total + unpick(o)
    out_ref[...] = total.astype(bf16)

    away = pl.ds(cap, (G - 1) * cap)
    await_bytes(outgoing.at[away], sent.at[0])
    if H > 1:
        await_bytes(rows.at[pl.ds(0, (H - 1) * G * cap)], sent.at[1])
        await_bytes(xout, sent.at[3])
    await_bytes(slab.at[0], sent.at[2])
    await_bytes(back.at[away], sent.at[4])


def per_device(queries, projection, vectors, bins, routes):
    G, NB = lax.axis_size("db"), lax.axis_size("blk")
    n, depth = queries.shape
    width = vectors.shape[1]
    cap = 2 * n // G
    sizes = [cap // 4] * 4 if cap % 64 == 0 else [cap]
    C = len(sizes)
    H = NB // 2
    tiles = width // TILE
    units = 5 if G == 4 and C == 4 else 1
    f32, bf16 = jnp.float32, jnp.bfloat16
    hbm = pl.BlockSpec(memory_space=pltpu.HBM)
    vmem = pl.BlockSpec(memory_space=pltpu.VMEM)
    dma = pltpu.SemaphoreType.DMA
    code = pl.pallas_call(
        functools.partial(kernel, G, NB, cap, tuple(sizes)),
        out_shape=pltpu.VMEM((n, BINS), bf16),
        in_specs=[hbm] * 5,
        out_specs=vmem,
        scratch_shapes=[
            pltpu.VMEM((n, depth), bf16),
            pltpu.VMEM(projection.shape, bf16),
            pltpu.VMEM((depth, width), bf16),
            pltpu.VMEM((1, width), jnp.int32),
            pltpu.VMEM((1, n), jnp.int32),
            pltpu.VMEM((2, tiles, depth, TILE), bf16),
            pltpu.VMEM((G * cap, n), bf16),
            pltpu.VMEM((G * cap, depth), bf16),
            pltpu.VMEM((H * G * cap, depth), bf16),
            pltpu.VMEM((G * cap, BINS), bf16),
            pltpu.VMEM((max(1, H - 1), G * cap, BINS), bf16),
            pltpu.VMEM((max(1, H - 1), G * cap, BINS), bf16),
            pltpu.VMEM((G * cap, BINS), bf16),
            pltpu.VMEM((G * cap, BINS), bf16),
            dma((5,)),
            dma((C, G - 1)),
            dma((units, max(1, H - 1))),
            dma((tiles,)),
            dma((units, max(1, H - 1))),
            dma((G - 1,)),
            dma((5,)),
        ],
        compiler_params=pltpu.CompilerParams(
            collective_id=0, has_side_effects=True, vmem_limit_bytes=60 * 1024 * 1024),
    )(queries, projection, vectors, bins.reshape(1, -1), routes.reshape(1, -1))
    return logit_scale * decode(code.astype(f32))


def solution(mesh):
    in_specs = (
        P(("parts", "db", "blk"), None),
        P(),
        P(None, ("parts", "db", "blk")),
        P(("parts", "db", "blk")),
        P(("parts", "db", "blk"), None),
    )
    out_specs = P(("parts", "db", "blk"), None)
    return jax.shard_map(
        per_device, mesh=mesh, in_specs=in_specs, out_specs=out_specs, check_vma=False
    )
```

```python
import functools

import jax
import jax.numpy as jnp
from jax import lax
from jax.experimental import pallas as pl
from jax.experimental.pallas import tpu as pltpu
from jax.sharding import PartitionSpec as P

BINS = 128
TILE = 256
logit_scale = 10.0
MESH = pl.DeviceIdType.MESH


CODE_SCALE = 2.0 ** 26


LEAVE = (
    (10, 11, 12, 13, 20, 30, 21, 31, 22, 32, 23, 33),
    (10, 11, 12, 13, 20, 30, 21, 31, 22, 32, 23, 33),
    (30, 10, 20, 11, 21, 12, 22, 13, 31, 23, 32, 33),
    (30, 10, 20, 11, 31, 12, 21, 13, 22, 32, 23, 33),
)
ARRIVE = (
    (10, 20, 21, 11, 12, 13, 30, 31, 32, 33, 22, 23),
    (10, 20, 11, 21, 22, 12, 30, 13, 31, 32, 33, 23),
    (30, 10, 11, 12, 13, 20, 21, 22, 23, 31, 32, 33),
    (30, 10, 11, 31, 12, 13, 20, 21, 22, 23, 32, 33),
)
LATE = 8


LEAST = -3.0e38


def encode(score):
    scaled = score * CODE_SCALE
    square = scaled * scaled
    fourth = square * square
    return jnp.where(score < 0, -fourth, fourth)


def decode(code):
    root = jnp.sqrt(jnp.sqrt(jnp.abs(code))) * (1.0 / CODE_SCALE)
    return jnp.where(code < 0, -root, root)


def kernel(
    G, NB, cap, sizes,
    q_hbm, p_hbm, v_hbm, b_hbm, r_hbm,
    out_ref,
    q_ref, p_ref, raw, bins_ref, routes_ref, slab, chooser, outgoing, rows, own, xout, xin, back, ans, ans2,
    load_sem, z_rs, x_rs, s_rs, xb_rs, zb_rs, yb_rs, sent,
):
    H = NB // 2
    C = len(sizes)
    n, depth = q_ref.shape
    width = raw.shape[1]
    tiles = width // TILE
    f32, bf16 = jnp.float32, jnp.bfloat16
    d = lax.axis_index("db")
    k = lax.axis_index("blk")

    load_r = pltpu.make_async_copy(r_hbm, routes_ref, load_sem.at[0])
    load_q = pltpu.make_async_copy(q_hbm, q_ref, load_sem.at[1])
    half = depth // 2
    load_p = [
        pltpu.make_async_copy(p_hbm.at[pl.ds(i * half, half)], p_ref.at[pl.ds(i * half, half)], load_sem.at[4 + i])
        for i in range(2)]
    load_b = pltpu.make_async_copy(b_hbm, bins_ref, load_sem.at[2])
    load_v = pltpu.make_async_copy(v_hbm, raw, load_sem.at[3])
    for load in (load_r, load_q, *load_p, load_b):
        load.start()

    direct = G == 4 and C == 4 and H == 2
    if direct:
        ans2[...] = jnp.full(ans2.shape, LEAST, bf16)
    barrier = pltpu.get_barrier_semaphore()
    for o in range(G - 1, 0, -1):
        pl.semaphore_signal(barrier, inc=1, device_id={"db": d ^ o}, device_id_type=MESH)
    for h in range(1, H):
        pl.semaphore_signal(barrier, inc=1, device_id={"blk": k ^ (2 * h)}, device_id_type=MESH)
    pl.semaphore_signal(barrier, inc=1, device_id={"blk": k ^ 1}, device_id_type=MESH)

    if G == 4 and C == 4:
        inner, odd = ((d + 1) // 2) % 2, k % 2

        def pick4(a, b, c, e):
            low = a if a == b else a + odd * (b - a)
            high = c if c == e else c + odd * (e - c)
            return low if low is high else low + inner * (high - low)

        def orders(*codes):
            lists = [[divmod(code, 10) for code in one] for one in codes]
            return [(pick4(*(o for o, _ in at)), pick4(*(c for _, c in at))) for at in zip(*lists, strict=True)]

        leave = orders(*LEAVE)
        order = orders(*ARRIVE)
        units = [[(0, c) for c in range(C)], order[:4], order[4:8], order[8:10], order[10:]]
    else:
        leave = [(o, c) for o in range(1, G) for c in range(C)]
        units = [[(o, c) for o in range(G) for c in range(C)]]
    rank = sizes[0]

    def fixed(start, multiple=16):
        return start if isinstance(start, int) else pl.multiple_of(start, multiple)

    def slots(o, c):
        return pl.ds(fixed(o * cap + c * rank), rank)

    def group(o):
        return pl.ds(fixed(o * cap), cap)

    def block(o, c, h=0, many=1):
        return pl.ds(fixed(o * (H * cap) + (c * H + h) * rank), many * rank)

    def span(u):
        return pl.ds(sum(len(v) for v in units[:u]) * rank, len(units[u]) * rank)

    def z_copy(o, c):
        return pltpu.make_async_remote_copy(
            src_ref=outgoing.at[slots(o, c)], dst_ref=rows.at[block(o, c)],
            send_sem=sent.at[0], recv_sem=z_rs.at[c, o - 1],
            device_id={"db": d ^ o}, device_id_type=MESH)

    def x_copy(u, o, c, h, step):
        return pltpu.make_async_remote_copy(
            src_ref=rows.at[block(o, c, h)], dst_ref=rows.at[block(o, c, h + step)],
            send_sem=sent.at[1], recv_sem=x_rs.at[u, h + step - 1],
            device_id={"blk": k ^ (2 * step)}, device_id_type=MESH)

    def s_copy(t):
        return pltpu.make_async_remote_copy(
            src_ref=slab.at[0, t], dst_ref=slab.at[1, t],
            send_sem=sent.at[2], recv_sem=s_rs.at[0],
            device_id={"blk": k ^ 1}, device_id_type=MESH)

    def xb_copy(u, h):
        return pltpu.make_async_remote_copy(
            src_ref=xout.at[h - 1, span(u)], dst_ref=xin.at[h - 1, span(u)],
            send_sem=sent.at[3], recv_sem=xb_rs.at[u, h - 1],
            device_id={"blk": k ^ (2 * h)}, device_id_type=MESH)

    def zb_copy(o, c):
        return pltpu.make_async_remote_copy(
            src_ref=back.at[slots(o, c)], dst_ref=ans.at[slots(o, c)],
            send_sem=sent.at[4], recv_sem=zb_rs.at[o - 1],
            device_id={"db": d ^ o}, device_id_type=MESH)

    def yb_copy(u, i):
        o, c = units[u][i]
        return pltpu.make_async_remote_copy(
            src_ref=xout.at[0, pl.ds((sum(len(v) for v in units[:u]) + i) * rank, rank)],
            dst_ref=ans2.at[slots(o - 2, c)],
            send_sem=sent.at[3], recv_sem=yb_rs.at[0],
            device_id={"db": d ^ o, "blk": k ^ 2}, device_id_type=MESH)

    def await_bytes(ref, sem):
        pltpu.make_async_copy(ref, ref, sem).wait()

    def local(o):
        return isinstance(o, int) and o == 0

    load_r.wait()
    target = routes_ref[...]
    pad = max(8, G)
    hot = jnp.where(lax.broadcasted_iota(jnp.int32, (pad, n), 0) == target, 1.0, 0.0)
    before = jnp.where(
        lax.broadcasted_iota(jnp.int32, (n, n), 0) < lax.broadcasted_iota(jnp.int32, (n, n), 1),
        1.0, 0.0).astype(bf16)
    earlier = jnp.dot(hot.astype(bf16), before, preferred_element_type=f32)
    slot = jnp.sum(hot * earlier, axis=0, keepdims=True).astype(jnp.int32)
    position = (target ^ d) * cap + slot

    def leave_local():
        for c in range(C):
            if H > 1:
                x_copy(0, 0, c, 0, 1).start()

    load_q.wait()
    load_v.start()
    picks = [
        jnp.where(
            lax.broadcasted_iota(jnp.int32, (cap, n), 0) + o * cap == position, 1.0, 0.0
        ).astype(bf16) for o in range(G)]
    for o in range(G):
        chooser[group(o), :] = picks[o]
    load_p[0].wait()
    projected = jnp.dot(q_ref[:, :half], p_ref[:half], preferred_element_type=f32)
    load_p[1].wait()
    projected += jnp.dot(q_ref[:, half:], p_ref[half:], preferred_element_type=f32)
    normed = (
        projected * lax.rsqrt(jnp.sum(projected * projected, axis=1, keepdims=True) + 1e-06)
    ).astype(bf16)
    chosen = jnp.dot(chooser[...], normed, preferred_element_type=f32).astype(bf16)
    outgoing[cap:, :] = chosen[cap:]
    for c in range(C):
        rows[block(0, c)] = chosen[c * rank:(c + 1) * rank]
    pl.semaphore_wait(barrier, G - 1 + H)
    z_copy(*leave[0]).start()
    leave_local()
    for o, c in leave[1:]:
        z_copy(o, c).start()

    def relay(u, i):
        o, c = units[u][i]
        z_copy(o, c).wait_recv()
        if H > 1:
            x_copy(u, o, c, 0, 1).start()

    load_b.wait()
    load_v.wait()
    bins = bins_ref[...]
    inner_mask = jnp.where(
        lax.broadcasted_iota(jnp.int32, (BINS, BINS), 0)
        < lax.broadcasted_iota(jnp.int32, (BINS, BINS), 1), 1.0, 0.0).astype(bf16)
    run = jnp.zeros((BINS, 1), f32)
    places = []
    for s in range(width // BINS):
        mine = bins[:, s * BINS:(s + 1) * BINS]
        hot = jnp.where(lax.broadcasted_iota(jnp.int32, (BINS, BINS), 0) == mine, 1.0, 0.0)
        earlier = jnp.dot(hot.astype(bf16), inner_mask, preferred_element_type=f32) + run
        turn = jnp.sum(hot * earlier, axis=0, keepdims=True).astype(jnp.int32)
        places.append(turn * BINS + mine)
        run = run + jnp.sum(hot, axis=1, keepdims=True)
    place = jnp.concatenate(places, axis=1)
    for t in range(tiles):
        move = jnp.where(
            lax.broadcasted_iota(jnp.int32, (TILE, width), 0) + t * TILE == place, 1.0, 0.0
        ).astype(bf16)
        slab[0, t] = lax.dot_general(
            raw[...], move, (((1,), (1,)), ((), ())), preferred_element_type=f32).astype(bf16)
        s_copy(t).start()

    def whole(u):
        return rows.at[pl.ds(0, len(units[u]) * rank)]

    def spread(u):
        step = 2
        while step < H:
            for h in range(step):
                if h >= step // 2:
                    await_bytes(whole(u), x_rs.at[u, h - 1])
                for o, c in units[u]:
                    x_copy(u, o, c, h, step).start()
            step *= 2

    def score(u):
        spread(u)
        for h in range(max(1, H // 2), H):
            await_bytes(whole(u), x_rs.at[u, h - 1])
        if u == 0:
            await_bytes(slab.at[1], s_rs.at[0])
        x = jnp.concatenate([rows[block(o, c, 0, H)] for o, c in units[u]], axis=0)
        best = None
        for side in range(2):
            for t in range(tiles):
                sc = jnp.dot(x, slab[side, t], preferred_element_type=f32)
                top = jnp.maximum(sc[:, :BINS], sc[:, BINS:])
                best = top if best is None else jnp.maximum(best, top)
        best = encode(best).astype(bf16)
        to = sum(len(v) for v in units[:u]) * rank
        for i in range(len(units[u])):
            for h in range(H):
                piece = best[(i * H + h) * rank:(i * H + h + 1) * rank]
                if h == 0:
                    own[pl.ds(to + i * rank, rank)] = piece
                else:
                    xout[h - 1, pl.ds(to + i * rank, rank)] = piece
        if direct and u >= 3:
            for i in range(len(units[u])):
                yb_copy(u, i).start()
        else:
            for h in range(1, H):
                xb_copy(u, h).start()

    def combine(u):
        total = own[span(u)]
        for h in range(1, 1 if direct and u >= 3 else H):
            xb_copy(u, h).wait_recv()
            total = jnp.maximum(total, xin[h - 1, span(u)])
        for i, (o, c) in enumerate(units[u]):
            piece = total[i * rank:(i + 1) * rank]
            if isinstance(o, int) and o == 0:
                ans[slots(0, c)] = piece
            else:
                back[slots(o, c)] = piece
                zb_copy(o, c).start()

    def unpick(o):
        if o:
            await_bytes(ans.at[group(o)], zb_rs.at[o - 1])
        found = ans[group(o)]
        if direct and o >= 2:
            found = jnp.maximum(found, ans2[group(o - 2)])
        return lax.dot_general(
            chooser[group(o), :], found, (((0,), (0,)), ((), ())), preferred_element_type=f32)

    if len(units) > 1:
        def relays(first, last):
            for p in range(first, last):
                if p < LATE:
                    relay(1 + p // 4, p % 4)
                else:
                    relay(3 + (p - LATE) // 2, p % 2)

        def finish():
            score(3)
            combine(3)
            combine(2)
            score(4)
            combine(4)
            combine(0)

        @pl.when(inner == 0)
        def _():
            relays(0, 4)
            score(0)
            relays(4, 8)
            score(1)
            relays(8, 11)
            score(2)
            relays(11, 12)
            combine(1)
            finish()

        @pl.when(inner == 1)
        def _():
            relays(0, 4)
            score(0)
            relays(4, 7)
            score(1)
            relays(7, 10)
            score(2)
            relays(10, 12)
            combine(1)
            finish()
    else:
        for i, (o, c) in enumerate(units[0]):
            if o:
                relay(0, i)
        score(0)
        combine(0)
    total = unpick(0)
    if G > 1:
        total = total + unpick(1)
    if direct:
        late = pick4(*(
            sum(code // 10 == o for o, at in ((2, 2 - i + j), (3, i + j)) for code in ARRIVE[at][LATE:])
            for i in (0, 2) for j in (0, 1)))
        for some in range(2 * C + 1):
            pl.when(late == some)(lambda some=some: await_bytes(ans2.at[pl.ds(0, some * rank)], yb_rs.at[0]))
    for o in range(2, G):
        total = total + unpick(o)
    out_ref[...] = total.astype(bf16)

    away = pl.ds(cap, (G - 1) * cap)
    await_bytes(outgoing.at[away], sent.at[0])
    if H > 1:
        await_bytes(rows.at[pl.ds(0, (H - 1) * G * cap)], sent.at[1])
        await_bytes(xout, sent.at[3])
    await_bytes(slab.at[0], sent.at[2])
    await_bytes(back.at[away], sent.at[4])


def per_device(queries, projection, vectors, bins, routes):
    G, NB = lax.axis_size("db"), lax.axis_size("blk")
    n, depth = queries.shape
    width = vectors.shape[1]
    cap = 2 * n // G
    sizes = [cap // 4] * 4 if cap % 64 == 0 else [cap]
    C = len(sizes)
    H = NB // 2
    tiles = width // TILE
    units = 5 if G == 4 and C == 4 else 1
    f32, bf16 = jnp.float32, jnp.bfloat16
    hbm = pl.BlockSpec(memory_space=pltpu.HBM)
    vmem = pl.BlockSpec(memory_space=pltpu.VMEM)
    dma = pltpu.SemaphoreType.DMA
    code = pl.pallas_call(
        functools.partial(kernel, G, NB, cap, tuple(sizes)),
        out_shape=pltpu.VMEM((n, BINS), bf16),
        in_specs=[hbm] * 5,
        out_specs=vmem,
        scratch_shapes=[
            pltpu.VMEM((n, depth), bf16),
            pltpu.VMEM(projection.shape, bf16),
            pltpu.VMEM((depth, width), bf16),
            pltpu.VMEM((1, width), jnp.int32),
            pltpu.VMEM((1, n), jnp.int32),
            pltpu.VMEM((2, tiles, depth, TILE), bf16),
            pltpu.VMEM((G * cap, n), bf16),
            pltpu.VMEM((G * cap, depth), bf16),
            pltpu.VMEM((H * G * cap, depth), bf16),
            pltpu.VMEM((G * cap, BINS), bf16),
            pltpu.VMEM((max(1, H - 1), G * cap, BINS), bf16),
            pltpu.VMEM((max(1, H - 1), G * cap, BINS), bf16),
            pltpu.VMEM((G * cap, BINS), bf16),
            pltpu.VMEM((G * cap, BINS), bf16),
            pltpu.VMEM((max(1, G // 2) * cap, BINS), bf16),
            dma((6,)),
            dma((C, G - 1)),
            dma((units, max(1, H - 1))),
            dma((1,)),
            dma((units, max(1, H - 1))),
            dma((G - 1,)),
            dma((1,)),
            dma((5,)),
        ],
        compiler_params=pltpu.CompilerParams(
            collective_id=0, has_side_effects=True, vmem_limit_bytes=60 * 1024 * 1024),
    )(queries, projection, vectors, bins.reshape(1, -1), routes.reshape(1, -1))
    return logit_scale * decode(code.astype(f32))


def solution(mesh):
    in_specs = (
        P(("parts", "db", "blk"), None),
        P(),
        P(None, ("parts", "db", "blk")),
        P(("parts", "db", "blk")),
        P(("parts", "db", "blk"), None),
    )
    out_specs = P(("parts", "db", "blk"), None)
    return jax.shard_map(
        per_device, mesh=mesh, in_specs=in_specs, out_specs=out_specs, check_vma=False
    )
```

```python
import functools

import jax
import jax.numpy as jnp
from jax import lax
from jax.experimental import pallas as pl
from jax.experimental.pallas import tpu as pltpu
from jax.sharding import PartitionSpec as P

BINS = 128
TILE = 256
logit_scale = 10.0
MESH = pl.DeviceIdType.MESH


CODE_SCALE = 2.0 ** 26


LEAVE = (
    (10, 11, 12, 13, 20, 30, 21, 31, 22, 32, 23, 33),
    (10, 11, 12, 13, 20, 30, 21, 31, 22, 32, 23, 33),
    (30, 10, 20, 11, 21, 12, 22, 13, 31, 23, 32, 33),
    (30, 10, 20, 11, 31, 12, 21, 13, 22, 32, 23, 33),
)
ARRIVE = (
    (10, 20, 21, 11, 12, 13, 30, 31, 32, 33, 22, 23),
    (10, 20, 11, 21, 22, 12, 30, 13, 31, 32, 33, 23),
    (30, 10, 11, 12, 13, 20, 21, 22, 23, 31, 32, 33),
    (30, 10, 11, 31, 12, 13, 20, 21, 22, 23, 32, 33),
)
LATE = (4, 4, 4, 4)


LEAST = -3.0e38


def encode(score):
    scaled = score * CODE_SCALE
    square = scaled * scaled
    fourth = square * square
    return jnp.where(score < 0, -fourth, fourth)


def decode(code):
    root = jnp.sqrt(jnp.sqrt(jnp.abs(code))) * (1.0 / CODE_SCALE)
    return jnp.where(code < 0, -root, root)


def kernel(
    G, NB, cap, sizes,
    q_hbm, p_hbm, v_hbm, b_hbm, r_hbm,
    out_ref,
    q_ref, p_ref, raw, bins_ref, routes_ref, slab, chooser, outgoing, rows, own, xout, xin, back, ans, ans2, chooser_t,
    load_sem, z_rs, x_rs, s_rs, xb_rs, zb_rs, yb_rs, sent,
):
    H = NB // 2
    C = len(sizes)
    n, depth = q_ref.shape
    width = raw.shape[1]
    tiles = width // TILE
    f32, bf16 = jnp.float32, jnp.bfloat16
    d = lax.axis_index("db")
    k = lax.axis_index("blk")

    load_r = pltpu.make_async_copy(r_hbm, routes_ref, load_sem.at[0])
    load_q = pltpu.make_async_copy(q_hbm, q_ref, load_sem.at[1])
    half = depth // 2
    load_p = [
        pltpu.make_async_copy(p_hbm.at[pl.ds(i * half, half)], p_ref.at[pl.ds(i * half, half)], load_sem.at[4 + i])
        for i in range(2)]
    load_b = pltpu.make_async_copy(b_hbm, bins_ref, load_sem.at[2])
    load_v = pltpu.make_async_copy(v_hbm, raw, load_sem.at[3])
    for load in (load_r, load_q, *load_p, load_b):
        load.start()

    direct = G == 4 and C == 4 and H == 2
    if direct:
        ans2[...] = jnp.full(ans2.shape, LEAST, bf16)
    barrier = pltpu.get_barrier_semaphore()
    for o in range(G - 1, 0, -1):
        pl.semaphore_signal(barrier, inc=1, device_id={"db": d ^ o}, device_id_type=MESH)
    for h in range(1, H):
        pl.semaphore_signal(barrier, inc=1, device_id={"blk": k ^ (2 * h)}, device_id_type=MESH)
    pl.semaphore_signal(barrier, inc=1, device_id={"blk": k ^ 1}, device_id_type=MESH)

    if G == 4 and C == 4:
        inner, odd = ((d + 1) // 2) % 2, k % 2

        def pick4(a, b, c, e):
            low = a if a == b else a + odd * (b - a)
            high = c if c == e else c + odd * (e - c)
            return low if low is high else low + inner * (high - low)

        def orders(*codes):
            lists = [[divmod(code, 10) for code in one] for one in codes]
            return [(pick4(*(o for o, _ in at)), pick4(*(c for _, c in at))) for at in zip(*lists, strict=True)]

        leave = orders(*LEAVE)
        order = orders(*ARRIVE)
        units = [[(0, c) for c in range(C)], order[:4], order[4:8], order[8:10], order[10:]]
    else:
        leave = [(o, c) for o in range(1, G) for c in range(C)]
        units = [[(o, c) for o in range(G) for c in range(C)]]
    rank = sizes[0]

    def fixed(start, multiple=16):
        return start if isinstance(start, int) else pl.multiple_of(start, multiple)

    def slots(o, c):
        return pl.ds(fixed(o * cap + c * rank), rank)

    def group(o):
        return pl.ds(fixed(o * cap), cap)

    def block(o, c, h=0, many=1):
        return pl.ds(fixed(o * (H * cap) + (c * H + h) * rank), many * rank)

    def span(u):
        return pl.ds(sum(len(v) for v in units[:u]) * rank, len(units[u]) * rank)

    def z_copy(o, c):
        return pltpu.make_async_remote_copy(
            src_ref=outgoing.at[slots(o, c)], dst_ref=rows.at[block(o, c)],
            send_sem=sent.at[0], recv_sem=z_rs.at[c, o - 1],
            device_id={"db": d ^ o}, device_id_type=MESH)

    def x_copy(u, o, c, h, step):
        return pltpu.make_async_remote_copy(
            src_ref=rows.at[block(o, c, h)], dst_ref=rows.at[block(o, c, h + step)],
            send_sem=sent.at[1], recv_sem=x_rs.at[u, h + step - 1],
            device_id={"blk": k ^ (2 * step)}, device_id_type=MESH)

    def s_copy(t):
        return pltpu.make_async_remote_copy(
            src_ref=slab.at[0, t], dst_ref=slab.at[1, t],
            send_sem=sent.at[2], recv_sem=s_rs.at[0],
            device_id={"blk": k ^ 1}, device_id_type=MESH)

    def xb_copy(u, h):
        return pltpu.make_async_remote_copy(
            src_ref=xout.at[h - 1, span(u)], dst_ref=xin.at[h - 1, span(u)],
            send_sem=sent.at[3], recv_sem=xb_rs.at[u, h - 1],
            device_id={"blk": k ^ (2 * h)}, device_id_type=MESH)

    def zb_copy(o, c):
        return pltpu.make_async_remote_copy(
            src_ref=back.at[slots(o, c)], dst_ref=ans.at[slots(o, c)],
            send_sem=sent.at[4], recv_sem=zb_rs.at[o - 1],
            device_id={"db": d ^ o}, device_id_type=MESH)

    def yb_copy(u, i):
        o, c = units[u][i]
        return pltpu.make_async_remote_copy(
            src_ref=xout.at[0, pl.ds((sum(len(v) for v in units[:u]) + i) * rank, rank)],
            dst_ref=ans2.at[slots(o - 1, c)],
            send_sem=sent.at[3], recv_sem=yb_rs.at[0],
            device_id={"db": d ^ o, "blk": k ^ 2}, device_id_type=MESH)

    def await_bytes(ref, sem):
        pltpu.make_async_copy(ref, ref, sem).wait()

    def local(o):
        return isinstance(o, int) and o == 0

    load_r.wait()
    target = routes_ref[...]
    pad = max(8, G)
    hot = jnp.where(lax.broadcasted_iota(jnp.int32, (pad, n), 0) == target, 1.0, 0.0)
    before = jnp.where(
        lax.broadcasted_iota(jnp.int32, (n, n), 0) < lax.broadcasted_iota(jnp.int32, (n, n), 1),
        1.0, 0.0).astype(bf16)
    earlier = jnp.dot(hot.astype(bf16), before, preferred_element_type=f32)
    slot = jnp.sum(hot * earlier, axis=0, keepdims=True).astype(jnp.int32)
    position = (target ^ d) * cap + slot

    def leave_local():
        for c in range(C):
            if H > 1:
                x_copy(0, 0, c, 0, 1).start()

    load_q.wait()
    load_v.start()
    picks = [
        jnp.where(
            lax.broadcasted_iota(jnp.int32, (cap, n), 0) + o * cap == position, 1.0, 0.0
        ).astype(bf16) for o in range(G)]
    for o in range(G):
        chooser[group(o), :] = picks[o]
    load_p[0].wait()
    projected = jnp.dot(q_ref[:, :half], p_ref[:half], preferred_element_type=f32)
    load_p[1].wait()
    projected += jnp.dot(q_ref[:, half:], p_ref[half:], preferred_element_type=f32)
    normed = (
        projected * lax.rsqrt(jnp.sum(projected * projected, axis=1, keepdims=True) + 1e-06)
    ).astype(bf16)
    chosen = jnp.dot(chooser[...], normed, preferred_element_type=f32).astype(bf16)
    outgoing[cap:, :] = chosen[cap:]
    for c in range(C):
        rows[block(0, c)] = chosen[c * rank:(c + 1) * rank]
    pl.semaphore_wait(barrier, G - 1 + H)
    z_copy(*leave[0]).start()
    leave_local()
    for o, c in leave[1:]:
        z_copy(o, c).start()

    def relay(u, i):
        o, c = units[u][i]
        z_copy(o, c).wait_recv()
        if H > 1:
            x_copy(u, o, c, 0, 1).start()

    load_b.wait()
    load_v.wait()
    bins = bins_ref[...]
    inner_mask = jnp.where(
        lax.broadcasted_iota(jnp.int32, (BINS, BINS), 0)
        < lax.broadcasted_iota(jnp.int32, (BINS, BINS), 1), 1.0, 0.0).astype(bf16)
    run = jnp.zeros((BINS, 1), f32)
    places = []
    for s in range(width // BINS):
        mine = bins[:, s * BINS:(s + 1) * BINS]
        hot = jnp.where(lax.broadcasted_iota(jnp.int32, (BINS, BINS), 0) == mine, 1.0, 0.0)
        earlier = jnp.dot(hot.astype(bf16), inner_mask, preferred_element_type=f32) + run
        turn = jnp.sum(hot * earlier, axis=0, keepdims=True).astype(jnp.int32)
        places.append(turn * BINS + mine)
        run = run + jnp.sum(hot, axis=1, keepdims=True)
    place = jnp.concatenate(places, axis=1)
    for t in range(tiles):
        move = jnp.where(
            lax.broadcasted_iota(jnp.int32, (TILE, width), 0) + t * TILE == place, 1.0, 0.0
        ).astype(bf16)
        slab[0, t] = lax.dot_general(
            raw[...], move, (((1,), (1,)), ((), ())), preferred_element_type=f32).astype(bf16)
        s_copy(t).start()

    def whole(u):
        return rows.at[pl.ds(0, len(units[u]) * rank)]

    def spread(u):
        step = 2
        while step < H:
            for h in range(step):
                if h >= step // 2:
                    await_bytes(whole(u), x_rs.at[u, h - 1])
                for o, c in units[u]:
                    x_copy(u, o, c, h, step).start()
            step *= 2

    def score(u, straight=False):
        spread(u)
        for h in range(max(1, H // 2), H):
            await_bytes(whole(u), x_rs.at[u, h - 1])
        if u == 0:
            await_bytes(slab.at[1], s_rs.at[0])
        x = jnp.concatenate([rows[block(o, c, 0, H)] for o, c in units[u]], axis=0)
        best = None
        for side in range(2):
            for t in range(tiles):
                sc = jnp.dot(x, slab[side, t], preferred_element_type=f32)
                top = jnp.maximum(sc[:, :BINS], sc[:, BINS:])
                best = top if best is None else jnp.maximum(best, top)
        best = encode(best).astype(bf16)
        to = sum(len(v) for v in units[:u]) * rank
        for i in range(len(units[u])):
            for h in range(H):
                piece = best[(i * H + h) * rank:(i * H + h + 1) * rank]
                if h == 0:
                    own[pl.ds(to + i * rank, rank)] = piece
                else:
                    xout[h - 1, pl.ds(to + i * rank, rank)] = piece
        if straight and direct:
            for i in range(len(units[u])):
                yb_copy(u, i).start()
        elif len(units) == 1:
            share(u)

    def share(u):
        for h in range(1, H):
            xb_copy(u, h).start()

    def combine(u, straight=False):
        total = own[span(u)]
        for h in range(1, 1 if straight and direct else H):
            xb_copy(u, h).wait_recv()
            total = jnp.maximum(total, xin[h - 1, span(u)])
        for i, (o, c) in enumerate(units[u]):
            piece = total[i * rank:(i + 1) * rank]
            if isinstance(o, int) and o == 0:
                ans[slots(0, c)] = piece
            else:
                back[slots(o, c)] = piece
                zb_copy(o, c).start()

    column = jnp.transpose(jnp.broadcast_to(position.astype(f32), (8, n)))[:, :1].astype(jnp.int32)
    chooser_t[...] = jnp.where(
        lax.broadcasted_iota(jnp.int32, (n, G * cap), 1) == column, 1.0, 0.0).astype(bf16)

    if len(units) > 1:
        def relays(first, last):
            for p in range(first, last):
                if p < 8:
                    relay(1 + p // 4, p % 4)
                else:
                    relay(3 + (p - 8) // 2, p % 2)

        def finish():
            score(3, True)
            combine(3, True)
            share(0)
            combine(1)
            score(4, True)
            combine(4, True)
            combine(0)

        @pl.when(inner == 0)
        def _():
            relays(0, 4)
            score(0)
            relays(4, 8)
            score(1)
            share(1)
            relays(8, 11)
            score(2, True)
            combine(2, True)
            relays(11, 12)
            finish()

        @pl.when(inner == 1)
        def _():
            relays(0, 4)
            score(0)
            relays(4, 7)
            score(1)
            share(1)
            relays(7, 12)
            score(2, True)
            combine(2, True)
            finish()
    else:
        for i, (o, c) in enumerate(units[0]):
            if o:
                relay(0, i)
        score(0)
        combine(0)
    total = jnp.dot(chooser_t[:, :cap], ans[:cap], preferred_element_type=f32)
    for o in range(1, G):
        await_bytes(ans.at[group(o)], zb_rs.at[o - 1])
    if direct:
        late = pick4(*(
            sum(code // 10 == o for o, at in ((1, 2 - i + j), (2, 2 - i + j), (3, i + j)) for code in ARRIVE[at][LATE[at]:])
            for i in (0, 2) for j in (0, 1)))
        for some in range(3 * C + 1):
            pl.when(late == some)(lambda some=some: await_bytes(ans2.at[pl.ds(0, some * rank)], yb_rs.at[0]))
    found = ans[cap:]
    if direct:
        found = jnp.maximum(found, ans2[...])
    total = total + jnp.dot(chooser_t[:, cap:], found, preferred_element_type=f32)
    out_ref[...] = total.astype(bf16)

    away = pl.ds(cap, (G - 1) * cap)
    await_bytes(outgoing.at[away], sent.at[0])
    if H > 1:
        await_bytes(rows.at[pl.ds(0, (H - 1) * G * cap)], sent.at[1])
        await_bytes(xout, sent.at[3])
    await_bytes(slab.at[0], sent.at[2])
    await_bytes(back.at[away], sent.at[4])


def per_device(queries, projection, vectors, bins, routes):
    G, NB = lax.axis_size("db"), lax.axis_size("blk")
    n, depth = queries.shape
    width = vectors.shape[1]
    cap = 2 * n // G
    sizes = [cap // 4] * 4 if cap % 64 == 0 else [cap]
    C = len(sizes)
    H = NB // 2
    tiles = width // TILE
    units = 5 if G == 4 and C == 4 else 1
    f32, bf16 = jnp.float32, jnp.bfloat16
    hbm = pl.BlockSpec(memory_space=pltpu.HBM)
    vmem = pl.BlockSpec(memory_space=pltpu.VMEM)
    dma = pltpu.SemaphoreType.DMA
    code = pl.pallas_call(
        functools.partial(kernel, G, NB, cap, tuple(sizes)),
        out_shape=pltpu.VMEM((n, BINS), bf16),
        in_specs=[hbm] * 5,
        out_specs=vmem,
        scratch_shapes=[
            pltpu.VMEM((n, depth), bf16),
            pltpu.VMEM(projection.shape, bf16),
            pltpu.VMEM((depth, width), bf16),
            pltpu.VMEM((1, width), jnp.int32),
            pltpu.VMEM((1, n), jnp.int32),
            pltpu.VMEM((2, tiles, depth, TILE), bf16),
            pltpu.VMEM((G * cap, n), bf16),
            pltpu.VMEM((G * cap, depth), bf16),
            pltpu.VMEM((H * G * cap, depth), bf16),
            pltpu.VMEM((G * cap, BINS), bf16),
            pltpu.VMEM((max(1, H - 1), G * cap, BINS), bf16),
            pltpu.VMEM((max(1, H - 1), G * cap, BINS), bf16),
            pltpu.VMEM((G * cap, BINS), bf16),
            pltpu.VMEM((G * cap, BINS), bf16),
            pltpu.VMEM((max(1, G - 1) * cap, BINS), bf16),
            pltpu.VMEM((n, G * cap), bf16),
            dma((6,)),
            dma((C, G - 1)),
            dma((units, max(1, H - 1))),
            dma((1,)),
            dma((units, max(1, H - 1))),
            dma((G - 1,)),
            dma((1,)),
            dma((5,)),
        ],
        compiler_params=pltpu.CompilerParams(
            collective_id=0, has_side_effects=True, vmem_limit_bytes=60 * 1024 * 1024),
    )(queries, projection, vectors, bins.reshape(1, -1), routes.reshape(1, -1))
    return logit_scale * decode(code.astype(f32))


def solution(mesh):
    in_specs = (
        P(("parts", "db", "blk"), None),
        P(),
        P(None, ("parts", "db", "blk")),
        P(("parts", "db", "blk")),
        P(("parts", "db", "blk"), None),
    )
    out_specs = P(("parts", "db", "blk"), None)
    return jax.shard_map(
        per_device, mesh=mesh, in_specs=in_specs, out_specs=out_specs, check_vma=False
    )
```

```python
import functools

import jax
import jax.numpy as jnp
from jax import lax
from jax.experimental import pallas as pl
from jax.experimental.pallas import tpu as pltpu
from jax.sharding import PartitionSpec as P

BINS = 128
TILE = 256
logit_scale = 10.0
MESH = pl.DeviceIdType.MESH


CODE_SCALE = 2.0 ** 26


LEAVE = (
    (10, 11, 12, 13, 20, 30, 21, 31, 22, 32, 23, 33),
    (10, 11, 12, 13, 20, 30, 21, 31, 22, 32, 23, 33),
    (30, 10, 20, 11, 21, 12, 22, 13, 31, 23, 32, 33),
    (30, 10, 20, 11, 31, 12, 21, 13, 22, 32, 23, 33),
)
ARRIVE = (
    (10, 20, 21, 11, 12, 13, 30, 31, 32, 33, 22, 23),
    (10, 20, 11, 21, 22, 12, 30, 13, 31, 32, 33, 23),
    (10, 11, 12, 13, 20, 21, 22, 23, 30, 31, 32, 33),
    (10, 11, 12, 13, 20, 21, 22, 23, 30, 31, 32, 33),
)
LATE = (4, 4, 4, 4)


LEAST = -3.0e38


def encode(score):
    scaled = score * CODE_SCALE
    square = scaled * scaled
    fourth = square * square
    return jnp.where(score < 0, -fourth, fourth)


def decode(code):
    root = jnp.sqrt(jnp.sqrt(jnp.abs(code))) * (1.0 / CODE_SCALE)
    return jnp.where(code < 0, -root, root)


def kernel(
    G, NB, cap, sizes,
    q_hbm, p_hbm, v_hbm, b_hbm, r_hbm,
    out_ref,
    q_ref, p_ref, raw, bins_ref, routes_ref, slab, chooser, outgoing, rows, own, xout, xin, back, ans, ans2, chooser_t,
    load_sem, z_rs, x_rs, s_rs, xb_rs, zb_rs, yb_rs, sent,
):
    H = NB // 2
    C = len(sizes)
    n, depth = q_ref.shape
    width = raw.shape[1]
    tiles = width // TILE
    f32, bf16 = jnp.float32, jnp.bfloat16
    d = lax.axis_index("db")
    k = lax.axis_index("blk")

    load_r = pltpu.make_async_copy(r_hbm, routes_ref, load_sem.at[0])
    load_q = pltpu.make_async_copy(q_hbm, q_ref, load_sem.at[1])
    half = depth // 2
    load_p = [
        pltpu.make_async_copy(p_hbm.at[pl.ds(i * half, half)], p_ref.at[pl.ds(i * half, half)], load_sem.at[4 + i])
        for i in range(2)]
    load_b = pltpu.make_async_copy(b_hbm, bins_ref, load_sem.at[2])
    load_v = pltpu.make_async_copy(v_hbm, raw, load_sem.at[3])
    for load in (load_r, load_q, *load_p, load_b):
        load.start()

    direct = G == 4 and C == 4 and H == 2
    if direct:
        ans2[...] = jnp.full(ans2.shape, LEAST, bf16)
    barrier = pltpu.get_barrier_semaphore()
    for o in range(G - 1, 0, -1):
        pl.semaphore_signal(barrier, inc=1, device_id={"db": d ^ o}, device_id_type=MESH)
    for h in range(1, H):
        pl.semaphore_signal(barrier, inc=1, device_id={"blk": k ^ (2 * h)}, device_id_type=MESH)
    pl.semaphore_signal(barrier, inc=1, device_id={"blk": k ^ 1}, device_id_type=MESH)

    if G == 4 and C == 4:
        inner, odd = ((d + 1) // 2) % 2, k % 2

        def pick4(a, b, c, e):
            low = a if a == b else a + odd * (b - a)
            high = c if c == e else c + odd * (e - c)
            return low if low is high else low + inner * (high - low)

        def orders(*codes):
            lists = [[divmod(code, 10) for code in one] for one in codes]
            return [(pick4(*(o for o, _ in at)), pick4(*(c for _, c in at))) for at in zip(*lists, strict=True)]

        leave = orders(*LEAVE)
        order = orders(*ARRIVE)
        units = [[(0, c) for c in range(C)], order[:4], order[4:8], order[8:10], order[10:]]
    else:
        leave = [(o, c) for o in range(1, G) for c in range(C)]
        units = [[(o, c) for o in range(G) for c in range(C)]]
    rank = sizes[0]

    def fixed(start, multiple=16):
        return start if isinstance(start, int) else pl.multiple_of(start, multiple)

    def slots(o, c):
        return pl.ds(fixed(o * cap + c * rank), rank)

    def group(o):
        return pl.ds(fixed(o * cap), cap)

    def block(o, c, h=0, many=1):
        return pl.ds(fixed(o * (H * cap) + (c * H + h) * rank), many * rank)

    def span(u):
        return pl.ds(sum(len(v) for v in units[:u]) * rank, len(units[u]) * rank)

    def z_copy(o, c):
        return pltpu.make_async_remote_copy(
            src_ref=outgoing.at[slots(o, c)], dst_ref=rows.at[block(o, c)],
            send_sem=sent.at[0], recv_sem=z_rs.at[c, o - 1],
            device_id={"db": d ^ o}, device_id_type=MESH)

    def x_copy(u, o, c, h, step):
        return pltpu.make_async_remote_copy(
            src_ref=rows.at[block(o, c, h)], dst_ref=rows.at[block(o, c, h + step)],
            send_sem=sent.at[1], recv_sem=x_rs.at[u, h + step - 1],
            device_id={"blk": k ^ (2 * step)}, device_id_type=MESH)

    def s_copy(t):
        return pltpu.make_async_remote_copy(
            src_ref=slab.at[0, t], dst_ref=slab.at[1, t],
            send_sem=sent.at[2], recv_sem=s_rs.at[0],
            device_id={"blk": k ^ 1}, device_id_type=MESH)

    def xb_copy(u, h):
        return pltpu.make_async_remote_copy(
            src_ref=xout.at[h - 1, span(u)], dst_ref=xin.at[h - 1, span(u)],
            send_sem=sent.at[3], recv_sem=xb_rs.at[u, h - 1],
            device_id={"blk": k ^ (2 * h)}, device_id_type=MESH)

    def zb_copy(o, c):
        return pltpu.make_async_remote_copy(
            src_ref=back.at[slots(o, c)], dst_ref=ans.at[slots(o, c)],
            send_sem=sent.at[4], recv_sem=zb_rs.at[o - 1],
            device_id={"db": d ^ o}, device_id_type=MESH)

    def yb_copy(u, i):
        o, c = units[u][i]
        return pltpu.make_async_remote_copy(
            src_ref=xout.at[0, pl.ds((sum(len(v) for v in units[:u]) + i) * rank, rank)],
            dst_ref=ans2.at[slots(o - 1, c)],
            send_sem=sent.at[3], recv_sem=yb_rs.at[0],
            device_id={"db": d ^ o, "blk": k ^ 2}, device_id_type=MESH)

    def await_bytes(ref, sem):
        pltpu.make_async_copy(ref, ref, sem).wait()

    def local(o):
        return isinstance(o, int) and o == 0

    load_r.wait()
    target = routes_ref[...]
    pad = max(8, G)
    hot = jnp.where(lax.broadcasted_iota(jnp.int32, (pad, n), 0) == target, 1.0, 0.0)
    before = jnp.where(
        lax.broadcasted_iota(jnp.int32, (n, n), 0) < lax.broadcasted_iota(jnp.int32, (n, n), 1),
        1.0, 0.0).astype(bf16)
    earlier = jnp.dot(hot.astype(bf16), before, preferred_element_type=f32)
    slot = jnp.sum(hot * earlier, axis=0, keepdims=True).astype(jnp.int32)
    position = (target ^ d) * cap + slot

    def leave_local():
        for c in range(C):
            if H > 1:
                x_copy(0, 0, c, 0, 1).start()

    load_q.wait()
    load_v.start()
    picks = [
        jnp.where(
            lax.broadcasted_iota(jnp.int32, (cap, n), 0) + o * cap == position, 1.0, 0.0
        ).astype(bf16) for o in range(G)]
    for o in range(G):
        chooser[group(o), :] = picks[o]
    load_p[0].wait()
    projected = jnp.dot(q_ref[:, :half], p_ref[:half], preferred_element_type=f32)
    load_p[1].wait()
    projected += jnp.dot(q_ref[:, half:], p_ref[half:], preferred_element_type=f32)
    normed = (
        projected * lax.rsqrt(jnp.sum(projected * projected, axis=1, keepdims=True) + 1e-06)
    ).astype(bf16)
    chosen = jnp.dot(chooser[...], normed, preferred_element_type=f32).astype(bf16)
    outgoing[cap:, :] = chosen[cap:]
    for c in range(C):
        rows[block(0, c)] = chosen[c * rank:(c + 1) * rank]
    pl.semaphore_wait(barrier, G - 1 + H)
    z_copy(*leave[0]).start()
    leave_local()
    for o, c in leave[1:]:
        z_copy(o, c).start()

    def relay(u, i):
        o, c = units[u][i]
        z_copy(o, c).wait_recv()
        if H > 1:
            x_copy(u, o, c, 0, 1).start()

    load_b.wait()
    load_v.wait()
    bins = bins_ref[...]
    inner_mask = jnp.where(
        lax.broadcasted_iota(jnp.int32, (BINS, BINS), 0)
        < lax.broadcasted_iota(jnp.int32, (BINS, BINS), 1), 1.0, 0.0).astype(bf16)
    run = jnp.zeros((BINS, 1), f32)
    places = []
    for s in range(width // BINS):
        mine = bins[:, s * BINS:(s + 1) * BINS]
        hot = jnp.where(lax.broadcasted_iota(jnp.int32, (BINS, BINS), 0) == mine, 1.0, 0.0)
        earlier = jnp.dot(hot.astype(bf16), inner_mask, preferred_element_type=f32) + run
        turn = jnp.sum(hot * earlier, axis=0, keepdims=True).astype(jnp.int32)
        places.append(turn * BINS + mine)
        run = run + jnp.sum(hot, axis=1, keepdims=True)
    place = jnp.concatenate(places, axis=1)
    for t in range(tiles):
        move = jnp.where(
            lax.broadcasted_iota(jnp.int32, (TILE, width), 0) + t * TILE == place, 1.0, 0.0
        ).astype(bf16)
        slab[0, t] = lax.dot_general(
            raw[...], move, (((1,), (1,)), ((), ())), preferred_element_type=f32).astype(bf16)
        s_copy(t).start()

    def whole(u):
        return rows.at[pl.ds(0, len(units[u]) * rank)]

    def spread(u):
        step = 2
        while step < H:
            for h in range(step):
                if h >= step // 2:
                    await_bytes(whole(u), x_rs.at[u, h - 1])
                for o, c in units[u]:
                    x_copy(u, o, c, h, step).start()
            step *= 2

    def score(u, straight=False):
        spread(u)
        for h in range(max(1, H // 2), H):
            await_bytes(whole(u), x_rs.at[u, h - 1])
        if u == 0:
            await_bytes(slab.at[1], s_rs.at[0])
        x = jnp.concatenate([rows[block(o, c, 0, H)] for o, c in units[u]], axis=0)
        best = None
        for side in range(2):
            for t in range(tiles):
                sc = jnp.dot(x, slab[side, t], preferred_element_type=f32)
                top = jnp.maximum(sc[:, :BINS], sc[:, BINS:])
                best = top if best is None else jnp.maximum(best, top)
        best = encode(best).astype(bf16)
        to = sum(len(v) for v in units[:u]) * rank
        for i in range(len(units[u])):
            for h in range(H):
                piece = best[(i * H + h) * rank:(i * H + h + 1) * rank]
                if h == 0:
                    own[pl.ds(to + i * rank, rank)] = piece
                else:
                    xout[h - 1, pl.ds(to + i * rank, rank)] = piece
        if straight and direct:
            for i in range(len(units[u])):
                yb_copy(u, i).start()
        elif len(units) == 1:
            share(u)

    def share(u):
        for h in range(1, H):
            xb_copy(u, h).start()

    def combine(u, straight=False):
        total = own[span(u)]
        for h in range(1, 1 if straight and direct else H):
            xb_copy(u, h).wait_recv()
            total = jnp.maximum(total, xin[h - 1, span(u)])
        for i, (o, c) in enumerate(units[u]):
            piece = total[i * rank:(i + 1) * rank]
            if isinstance(o, int) and o == 0:
                ans[slots(0, c)] = piece
            else:
                back[slots(o, c)] = piece
                zb_copy(o, c).start()

    column = jnp.transpose(jnp.broadcast_to(position.astype(f32), (8, n)))[:, :1].astype(jnp.int32)
    chooser_t[...] = jnp.where(
        lax.broadcasted_iota(jnp.int32, (n, G * cap), 1) == column, 1.0, 0.0).astype(bf16)

    if len(units) > 1:
        def relays(first, last):
            for p in range(first, last):
                if p < 8:
                    relay(1 + p // 4, p % 4)
                else:
                    relay(3 + (p - 8) // 2, p % 2)

        def finish(last=()):
            score(3, True)
            combine(3, True)
            share(0)
            for u in last:
                combine(u)
            score(4, True)
            combine(4, True)
            combine(0)

        @pl.when(inner == 0)
        def _():
            relays(0, 4)
            score(0)
            relays(4, 8)
            score(1)
            share(1)
            relays(8, 11)
            score(2, True)
            combine(2, True)
            relays(11, 12)
            finish((1,))

        @pl.when(inner == 1)
        def _():
            relays(8, 9)
            relays(0, 4)
            score(0)
            relays(4, 7)
            score(1)
            share(1)
            relays(7, 8)
            relays(9, 10)
            combine(1)
            relays(10, 12)
            score(2, True)
            combine(2, True)
            finish()
    else:
        for i, (o, c) in enumerate(units[0]):
            if o:
                relay(0, i)
        score(0)
        combine(0)
    total = jnp.dot(chooser_t[:, :cap], ans[:cap], preferred_element_type=f32)
    for o in range(1, G):
        await_bytes(ans.at[group(o)], zb_rs.at[o - 1])
    if direct:
        late = pick4(*(
            sum(code // 10 == o for o, at in ((1, 2 - i + j), (2, 2 - i + j), (3, i + j)) for code in ARRIVE[at][LATE[at]:])
            for i in (0, 2) for j in (0, 1)))
        for some in range(3 * C + 1):
            pl.when(late == some)(lambda some=some: await_bytes(ans2.at[pl.ds(0, some * rank)], yb_rs.at[0]))
    found = ans[cap:]
    if direct:
        found = jnp.maximum(found, ans2[...])
    total = total + jnp.dot(chooser_t[:, cap:], found, preferred_element_type=f32)
    out_ref[...] = total.astype(bf16)

    away = pl.ds(cap, (G - 1) * cap)
    await_bytes(outgoing.at[away], sent.at[0])
    if H > 1:
        await_bytes(rows.at[pl.ds(0, (H - 1) * G * cap)], sent.at[1])
        await_bytes(xout, sent.at[3])
    await_bytes(slab.at[0], sent.at[2])
    await_bytes(back.at[away], sent.at[4])


def per_device(queries, projection, vectors, bins, routes):
    G, NB = lax.axis_size("db"), lax.axis_size("blk")
    n, depth = queries.shape
    width = vectors.shape[1]
    cap = 2 * n // G
    sizes = [cap // 4] * 4 if cap % 64 == 0 else [cap]
    C = len(sizes)
    H = NB // 2
    tiles = width // TILE
    units = 5 if G == 4 and C == 4 else 1
    f32, bf16 = jnp.float32, jnp.bfloat16
    hbm = pl.BlockSpec(memory_space=pltpu.HBM)
    vmem = pl.BlockSpec(memory_space=pltpu.VMEM)
    dma = pltpu.SemaphoreType.DMA
    code = pl.pallas_call(
        functools.partial(kernel, G, NB, cap, tuple(sizes)),
        out_shape=pltpu.VMEM((n, BINS), bf16),
        in_specs=[hbm] * 5,
        out_specs=vmem,
        scratch_shapes=[
            pltpu.VMEM((n, depth), bf16),
            pltpu.VMEM(projection.shape, bf16),
            pltpu.VMEM((depth, width), bf16),
            pltpu.VMEM((1, width), jnp.int32),
            pltpu.VMEM((1, n), jnp.int32),
            pltpu.VMEM((2, tiles, depth, TILE), bf16),
            pltpu.VMEM((G * cap, n), bf16),
            pltpu.VMEM((G * cap, depth), bf16),
            pltpu.VMEM((H * G * cap, depth), bf16),
            pltpu.VMEM((G * cap, BINS), bf16),
            pltpu.VMEM((max(1, H - 1), G * cap, BINS), bf16),
            pltpu.VMEM((max(1, H - 1), G * cap, BINS), bf16),
            pltpu.VMEM((G * cap, BINS), bf16),
            pltpu.VMEM((G * cap, BINS), bf16),
            pltpu.VMEM((max(1, G - 1) * cap, BINS), bf16),
            pltpu.VMEM((n, G * cap), bf16),
            dma((6,)),
            dma((C, G - 1)),
            dma((units, max(1, H - 1))),
            dma((1,)),
            dma((units, max(1, H - 1))),
            dma((G - 1,)),
            dma((1,)),
            dma((5,)),
        ],
        compiler_params=pltpu.CompilerParams(
            collective_id=0, has_side_effects=True, vmem_limit_bytes=60 * 1024 * 1024),
    )(queries, projection, vectors, bins.reshape(1, -1), routes.reshape(1, -1))
    return logit_scale * decode(code.astype(f32))


def solution(mesh):
    in_specs = (
        P(("parts", "db", "blk"), None),
        P(),
        P(None, ("parts", "db", "blk")),
        P(("parts", "db", "blk")),
        P(("parts", "db", "blk"), None),
    )
    out_specs = P(("parts", "db", "blk"), None)
    return jax.shard_map(
        per_device, mesh=mesh, in_specs=in_specs, out_specs=out_specs, check_vma=False
    )
```

```python
import functools

import jax
import jax.numpy as jnp
from jax import lax
from jax.experimental import pallas as pl
from jax.experimental.pallas import tpu as pltpu
from jax.sharding import PartitionSpec as P

BINS = 128
TILE = 256
logit_scale = 10.0
MESH = pl.DeviceIdType.MESH


CODE_SCALE = 2.0 ** 26


LEAVE = (
    (10, 11, 12, 13, 20, 30, 21, 31, 22, 32, 23, 33),
    (10, 11, 12, 13, 20, 30, 21, 31, 22, 32, 23, 33),
    (30, 10, 20, 11, 21, 12, 22, 13, 23, 31, 32, 33),
    (30, 10, 20, 11, 31, 12, 21, 13, 22, 32, 23, 33),
)
ARRIVE = (
    (10, 20, 21, 11, 12, 13, 30, 31, 32, 33, 22, 23),
    (10, 20, 11, 21, 22, 12, 30, 13, 31, 32, 33, 23),
    (10, 11, 12, 13, 20, 21, 22, 23, 30, 31, 32, 33),
    (10, 11, 12, 13, 20, 21, 22, 23, 30, 31, 32, 33),
)
LATE = (4, 4, 4, 4)


LEAST = -3.0e38


def encode(score):
    scaled = score * CODE_SCALE
    square = scaled * scaled
    fourth = square * square
    return jnp.where(score < 0, -fourth, fourth)


def decode(code):
    root = jnp.sqrt(jnp.sqrt(jnp.abs(code))) * (1.0 / CODE_SCALE)
    return jnp.where(code < 0, -root, root)


def kernel(
    G, NB, cap, sizes,
    q_hbm, p_hbm, v_hbm, b_hbm, r_hbm,
    out_ref,
    q_ref, p_ref, raw, bins_ref, routes_ref, slab, chooser, outgoing, rows, own, xout, xin, back, ans, ans2, chooser_t,
    load_sem, z_rs, x_rs, s_rs, xb_rs, zb_rs, yb_rs, sent,
):
    H = NB // 2
    C = len(sizes)
    n, depth = q_ref.shape
    width = raw.shape[1]
    tiles = width // TILE
    f32, bf16 = jnp.float32, jnp.bfloat16
    d = lax.axis_index("db")
    k = lax.axis_index("blk")

    load_r = pltpu.make_async_copy(r_hbm, routes_ref, load_sem.at[0])
    load_q = pltpu.make_async_copy(q_hbm, q_ref, load_sem.at[1])
    half = depth // 2
    load_p = [
        pltpu.make_async_copy(p_hbm.at[pl.ds(i * half, half)], p_ref.at[pl.ds(i * half, half)], load_sem.at[4 + i])
        for i in range(2)]
    load_b = pltpu.make_async_copy(b_hbm, bins_ref, load_sem.at[2])
    load_v = pltpu.make_async_copy(v_hbm, raw, load_sem.at[3])
    for load in (load_r, load_q, *load_p, load_b):
        load.start()

    direct = G == 4 and C == 4 and H == 2
    if direct:
        ans2[...] = jnp.full(ans2.shape, LEAST, bf16)
    barrier = pltpu.get_barrier_semaphore()
    for o in range(G - 1, 0, -1):
        pl.semaphore_signal(barrier, inc=1, device_id={"db": d ^ o}, device_id_type=MESH)
    for h in range(1, H):
        pl.semaphore_signal(barrier, inc=1, device_id={"blk": k ^ (2 * h)}, device_id_type=MESH)
    pl.semaphore_signal(barrier, inc=1, device_id={"blk": k ^ 1}, device_id_type=MESH)

    if G == 4 and C == 4:
        inner, odd = ((d + 1) // 2) % 2, k % 2

        def pick4(a, b, c, e):
            low = a if a == b else a + odd * (b - a)
            high = c if c == e else c + odd * (e - c)
            return low if low is high else low + inner * (high - low)

        def orders(*codes):
            lists = [[divmod(code, 10) for code in one] for one in codes]
            return [(pick4(*(o for o, _ in at)), pick4(*(c for _, c in at))) for at in zip(*lists, strict=True)]

        leave = orders(*LEAVE)
        order = orders(*ARRIVE)
        units = [[(0, c) for c in range(C)], order[:4], order[4:8], order[8:10], order[10:]]
    else:
        leave = [(o, c) for o in range(1, G) for c in range(C)]
        units = [[(o, c) for o in range(G) for c in range(C)]]
    rank = sizes[0]

    def fixed(start, multiple=16):
        return start if isinstance(start, int) else pl.multiple_of(start, multiple)

    def slots(o, c):
        return pl.ds(fixed(o * cap + c * rank), rank)

    def group(o):
        return pl.ds(fixed(o * cap), cap)

    def block(o, c, h=0, many=1):
        return pl.ds(fixed(o * (H * cap) + (c * H + h) * rank), many * rank)

    def span(u):
        return pl.ds(sum(len(v) for v in units[:u]) * rank, len(units[u]) * rank)

    def z_copy(o, c):
        return pltpu.make_async_remote_copy(
            src_ref=outgoing.at[slots(o, c)], dst_ref=rows.at[block(o, c)],
            send_sem=sent.at[0], recv_sem=z_rs.at[c, o - 1],
            device_id={"db": d ^ o}, device_id_type=MESH)

    def x_copy(u, o, c, h, step):
        return pltpu.make_async_remote_copy(
            src_ref=rows.at[block(o, c, h)], dst_ref=rows.at[block(o, c, h + step)],
            send_sem=sent.at[1], recv_sem=x_rs.at[u, h + step - 1],
            device_id={"blk": k ^ (2 * step)}, device_id_type=MESH)

    def s_copy(t):
        return pltpu.make_async_remote_copy(
            src_ref=slab.at[0, t], dst_ref=slab.at[1, t],
            send_sem=sent.at[2], recv_sem=s_rs.at[0],
            device_id={"blk": k ^ 1}, device_id_type=MESH)

    def xb_copy(u, h):
        return pltpu.make_async_remote_copy(
            src_ref=xout.at[h - 1, span(u)], dst_ref=xin.at[h - 1, span(u)],
            send_sem=sent.at[3], recv_sem=xb_rs.at[u, h - 1],
            device_id={"blk": k ^ (2 * h)}, device_id_type=MESH)

    def zb_copy(o, c):
        return pltpu.make_async_remote_copy(
            src_ref=back.at[slots(o, c)], dst_ref=ans.at[slots(o, c)],
            send_sem=sent.at[4], recv_sem=zb_rs.at[o - 1],
            device_id={"db": d ^ o}, device_id_type=MESH)

    def yb_copy(u, i):
        o, c = units[u][i]
        return pltpu.make_async_remote_copy(
            src_ref=xout.at[0, pl.ds((sum(len(v) for v in units[:u]) + i) * rank, rank)],
            dst_ref=ans2.at[slots(o - 1, c)],
            send_sem=sent.at[3], recv_sem=yb_rs.at[0],
            device_id={"db": d ^ o, "blk": k ^ 2}, device_id_type=MESH)

    def await_bytes(ref, sem):
        pltpu.make_async_copy(ref, ref, sem).wait()

    def local(o):
        return isinstance(o, int) and o == 0

    load_r.wait()
    target = routes_ref[...]
    pad = max(8, G)
    hot = jnp.where(lax.broadcasted_iota(jnp.int32, (pad, n), 0) == target, 1.0, 0.0)
    before = jnp.where(
        lax.broadcasted_iota(jnp.int32, (n, n), 0) < lax.broadcasted_iota(jnp.int32, (n, n), 1),
        1.0, 0.0).astype(bf16)
    earlier = jnp.dot(hot.astype(bf16), before, preferred_element_type=f32)
    slot = jnp.sum(hot * earlier, axis=0, keepdims=True).astype(jnp.int32)
    position = (target ^ d) * cap + slot

    def leave_local():
        for c in range(C):
            if H > 1:
                x_copy(0, 0, c, 0, 1).start()

    load_q.wait()
    picks = [
        jnp.where(
            lax.broadcasted_iota(jnp.int32, (cap, n), 0) + o * cap == position, 1.0, 0.0
        ).astype(bf16) for o in range(G)]
    for o in range(G):
        chooser[group(o), :] = picks[o]
    load_p[0].wait()
    projected = jnp.dot(q_ref[:, :half], p_ref[:half], preferred_element_type=f32)
    load_p[1].wait()
    load_v.start()
    projected += jnp.dot(q_ref[:, half:], p_ref[half:], preferred_element_type=f32)
    normed = (
        projected * lax.rsqrt(jnp.sum(projected * projected, axis=1, keepdims=True) + 1e-06)
    ).astype(bf16)
    chosen = jnp.dot(chooser[...], normed, preferred_element_type=f32).astype(bf16)
    outgoing[cap:, :] = chosen[cap:]
    for c in range(C):
        rows[block(0, c)] = chosen[c * rank:(c + 1) * rank]
    pl.semaphore_wait(barrier, G - 1 + H)
    z_copy(*leave[0]).start()
    leave_local()
    for o, c in leave[1:]:
        z_copy(o, c).start()

    def relay(u, i):
        o, c = units[u][i]
        z_copy(o, c).wait_recv()
        if H > 1:
            x_copy(u, o, c, 0, 1).start()

    load_b.wait()
    load_v.wait()
    bins = bins_ref[...]
    inner_mask = jnp.where(
        lax.broadcasted_iota(jnp.int32, (BINS, BINS), 0)
        < lax.broadcasted_iota(jnp.int32, (BINS, BINS), 1), 1.0, 0.0).astype(bf16)
    run = jnp.zeros((BINS, 1), f32)
    places = []
    for s in range(width // BINS):
        mine = bins[:, s * BINS:(s + 1) * BINS]
        hot = jnp.where(lax.broadcasted_iota(jnp.int32, (BINS, BINS), 0) == mine, 1.0, 0.0)
        earlier = jnp.dot(hot.astype(bf16), inner_mask, preferred_element_type=f32) + run
        turn = jnp.sum(hot * earlier, axis=0, keepdims=True).astype(jnp.int32)
        places.append(turn * BINS + mine)
        run = run + jnp.sum(hot, axis=1, keepdims=True)
    place = jnp.concatenate(places, axis=1)
    for t in range(tiles):
        move = jnp.where(
            lax.broadcasted_iota(jnp.int32, (TILE, width), 0) + t * TILE == place, 1.0, 0.0
        ).astype(bf16)
        slab[0, t] = lax.dot_general(
            raw[...], move, (((1,), (1,)), ((), ())), preferred_element_type=f32).astype(bf16)
        s_copy(t).start()

    def whole(u):
        return rows.at[pl.ds(0, len(units[u]) * rank)]

    def spread(u):
        step = 2
        while step < H:
            for h in range(step):
                if h >= step // 2:
                    await_bytes(whole(u), x_rs.at[u, h - 1])
                for o, c in units[u]:
                    x_copy(u, o, c, h, step).start()
            step *= 2

    def score(u, straight=False):
        spread(u)
        for h in range(max(1, H // 2), H):
            await_bytes(whole(u), x_rs.at[u, h - 1])
        if u == 0:
            await_bytes(slab.at[1], s_rs.at[0])
        x = jnp.concatenate([rows[block(o, c, 0, H)] for o, c in units[u]], axis=0)
        best = None
        for side in range(2):
            for t in range(tiles):
                sc = jnp.dot(x, slab[side, t], preferred_element_type=f32)
                top = jnp.maximum(sc[:, :BINS], sc[:, BINS:])
                best = top if best is None else jnp.maximum(best, top)
        best = encode(best).astype(bf16)
        to = sum(len(v) for v in units[:u]) * rank
        for i in range(len(units[u])):
            for h in range(H):
                piece = best[(i * H + h) * rank:(i * H + h + 1) * rank]
                if h == 0:
                    own[pl.ds(to + i * rank, rank)] = piece
                else:
                    xout[h - 1, pl.ds(to + i * rank, rank)] = piece
        if straight and direct:
            for i in range(len(units[u])):
                yb_copy(u, i).start()
        elif len(units) == 1:
            share(u)

    def share(u):
        for h in range(1, H):
            xb_copy(u, h).start()

    def combine(u, straight=False):
        total = own[span(u)]
        for h in range(1, 1 if straight and direct else H):
            xb_copy(u, h).wait_recv()
            total = jnp.maximum(total, xin[h - 1, span(u)])
        for i, (o, c) in enumerate(units[u]):
            piece = total[i * rank:(i + 1) * rank]
            if isinstance(o, int) and o == 0:
                ans[slots(0, c)] = piece
            else:
                back[slots(o, c)] = piece
                zb_copy(o, c).start()

    column = jnp.transpose(jnp.broadcast_to(position.astype(f32), (8, n)))[:, :1].astype(jnp.int32)
    chooser_t[...] = jnp.where(
        lax.broadcasted_iota(jnp.int32, (n, G * cap), 1) == column, 1.0, 0.0).astype(bf16)

    if len(units) > 1:
        def relays(first, last):
            for p in range(first, last):
                if p < 8:
                    relay(1 + p // 4, p % 4)
                else:
                    relay(3 + (p - 8) // 2, p % 2)

        def finish(last=()):
            score(3, True)
            combine(3, True)
            share(0)
            for u in last:
                combine(u)
            score(4, True)
            combine(4, True)
            combine(0)

        @pl.when(inner == 0)
        def _():
            relays(0, 4)
            score(0)
            relays(4, 8)
            score(1)
            share(1)
            relays(8, 11)
            score(2, True)
            combine(2, True)
            relays(11, 12)
            finish((1,))

        @pl.when(inner == 1)
        def _():
            relays(8, 9)
            relays(0, 4)
            score(0)
            relays(4, 7)
            score(1)
            share(1)
            relays(7, 8)
            relays(9, 10)
            combine(1)
            relays(10, 12)
            score(2, True)
            combine(2, True)
            finish()
    else:
        for i, (o, c) in enumerate(units[0]):
            if o:
                relay(0, i)
        score(0)
        combine(0)
    total = jnp.dot(chooser_t[:, :cap], ans[:cap], preferred_element_type=f32)
    for o in range(1, G):
        await_bytes(ans.at[group(o)], zb_rs.at[o - 1])
    if direct:
        late = pick4(*(
            sum(code // 10 == o for o, at in ((1, 2 - i + j), (2, 2 - i + j), (3, i + j)) for code in ARRIVE[at][LATE[at]:])
            for i in (0, 2) for j in (0, 1)))
        for some in range(3 * C + 1):
            pl.when(late == some)(lambda some=some: await_bytes(ans2.at[pl.ds(0, some * rank)], yb_rs.at[0]))
    found = ans[cap:]
    if direct:
        found = jnp.maximum(found, ans2[...])
    total = total + jnp.dot(chooser_t[:, cap:], found, preferred_element_type=f32)
    out_ref[...] = total.astype(bf16)

    away = pl.ds(cap, (G - 1) * cap)
    await_bytes(outgoing.at[away], sent.at[0])
    if H > 1:
        await_bytes(rows.at[pl.ds(0, (H - 1) * G * cap)], sent.at[1])
        await_bytes(xout, sent.at[3])
    await_bytes(slab.at[0], sent.at[2])
    await_bytes(back.at[away], sent.at[4])


def per_device(queries, projection, vectors, bins, routes):
    G, NB = lax.axis_size("db"), lax.axis_size("blk")
    n, depth = queries.shape
    width = vectors.shape[1]
    cap = 2 * n // G
    sizes = [cap // 4] * 4 if cap % 64 == 0 else [cap]
    C = len(sizes)
    H = NB // 2
    tiles = width // TILE
    units = 5 if G == 4 and C == 4 else 1
    f32, bf16 = jnp.float32, jnp.bfloat16
    hbm = pl.BlockSpec(memory_space=pltpu.HBM)
    vmem = pl.BlockSpec(memory_space=pltpu.VMEM)
    dma = pltpu.SemaphoreType.DMA
    code = pl.pallas_call(
        functools.partial(kernel, G, NB, cap, tuple(sizes)),
        out_shape=pltpu.VMEM((n, BINS), bf16),
        in_specs=[hbm] * 5,
        out_specs=vmem,
        scratch_shapes=[
            pltpu.VMEM((n, depth), bf16),
            pltpu.VMEM(projection.shape, bf16),
            pltpu.VMEM((depth, width), bf16),
            pltpu.VMEM((1, width), jnp.int32),
            pltpu.VMEM((1, n), jnp.int32),
            pltpu.VMEM((2, tiles, depth, TILE), bf16),
            pltpu.VMEM((G * cap, n), bf16),
            pltpu.VMEM((G * cap, depth), bf16),
            pltpu.VMEM((H * G * cap, depth), bf16),
            pltpu.VMEM((G * cap, BINS), bf16),
            pltpu.VMEM((max(1, H - 1), G * cap, BINS), bf16),
            pltpu.VMEM((max(1, H - 1), G * cap, BINS), bf16),
            pltpu.VMEM((G * cap, BINS), bf16),
            pltpu.VMEM((G * cap, BINS), bf16),
            pltpu.VMEM((max(1, G - 1) * cap, BINS), bf16),
            pltpu.VMEM((n, G * cap), bf16),
            dma((6,)),
            dma((C, G - 1)),
            dma((units, max(1, H - 1))),
            dma((1,)),
            dma((units, max(1, H - 1))),
            dma((G - 1,)),
            dma((1,)),
            dma((5,)),
        ],
        compiler_params=pltpu.CompilerParams(
            collective_id=0, has_side_effects=True, vmem_limit_bytes=60 * 1024 * 1024),
    )(queries, projection, vectors, bins.reshape(1, -1), routes.reshape(1, -1))
    return logit_scale * decode(code.astype(f32))


def solution(mesh):
    in_specs = (
        P(("parts", "db", "blk"), None),
        P(),
        P(None, ("parts", "db", "blk")),
        P(("parts", "db", "blk")),
        P(("parts", "db", "blk"), None),
    )
    out_specs = P(("parts", "db", "blk"), None)
    return jax.shard_map(
        per_device, mesh=mesh, in_specs=in_specs, out_specs=out_specs, check_vma=False
    )
```

```python
import functools

import jax
import jax.numpy as jnp
from jax import lax
from jax.experimental import pallas as pl
from jax.experimental.pallas import tpu as pltpu
from jax.sharding import PartitionSpec as P

BINS = 128
TILE = 256
logit_scale = 10.0
MESH = pl.DeviceIdType.MESH


CODE_SCALE = 2.0 ** 26


LEAVE = (
    (10, 11, 12, 13, 20, 30, 21, 31, 22, 32, 23, 33),
    (10, 11, 12, 13, 20, 30, 21, 31, 22, 32, 23, 33),
    (30, 10, 20, 11, 21, 12, 22, 13, 23, 31, 32, 33),
    (30, 10, 20, 11, 31, 12, 21, 13, 22, 32, 23, 33),
)
ARRIVE = (
    (10, 20, 21, 11, 12, 13, 30, 31, 32, 33, 22, 23),
    (10, 20, 11, 21, 22, 12, 30, 13, 31, 32, 33, 23),
    (10, 11, 12, 13, 20, 21, 22, 23, 30, 31, 32, 33),
    (10, 11, 12, 13, 20, 21, 22, 23, 30, 31, 32, 33),
)
LATE = (4, 4, 4, 4)


LEAST = -3.0e38


def encode(score):
    scaled = score * CODE_SCALE
    square = scaled * scaled
    fourth = square * square
    return jnp.where(score < 0, -fourth, fourth)


def decode(code):
    root = jnp.sqrt(jnp.sqrt(jnp.abs(code))) * (1.0 / CODE_SCALE)
    return jnp.where(code < 0, -root, root)


def kernel(
    G, NB, cap, sizes,
    q_hbm, p_hbm, v_hbm, b_hbm, r_hbm,
    out_ref,
    q_ref, p_ref, raw, bins_ref, routes_ref, slab, chooser, outgoing, rows, own, xout, xin, back, ans, ans2, chooser_t,
    load_sem, z_rs, x_rs, s_rs, xb_rs, zb_rs, yb_rs, sent,
):
    H = NB // 2
    C = len(sizes)
    n, depth = q_ref.shape
    width = raw.shape[1]
    tiles = width // TILE
    f32, bf16 = jnp.float32, jnp.bfloat16
    d = lax.axis_index("db")
    k = lax.axis_index("blk")

    load_r = pltpu.make_async_copy(r_hbm, routes_ref, load_sem.at[0])
    load_q = pltpu.make_async_copy(q_hbm, q_ref, load_sem.at[1])
    half = depth // 2
    load_p = [
        pltpu.make_async_copy(p_hbm.at[pl.ds(i * half, half)], p_ref.at[pl.ds(i * half, half)], load_sem.at[4 + i])
        for i in range(2)]
    load_b = pltpu.make_async_copy(b_hbm, bins_ref, load_sem.at[2])
    load_v = pltpu.make_async_copy(v_hbm, raw, load_sem.at[3])
    for load in (load_r, load_q, *load_p, load_b):
        load.start()

    direct = G == 4 and C == 4 and H == 2
    if direct:
        ans2[...] = jnp.full(ans2.shape, LEAST, bf16)
    barrier = pltpu.get_barrier_semaphore()
    for o in range(G - 1, 0, -1):
        pl.semaphore_signal(barrier, inc=1, device_id={"db": d ^ o}, device_id_type=MESH)
    for h in range(1, H):
        pl.semaphore_signal(barrier, inc=1, device_id={"blk": k ^ (2 * h)}, device_id_type=MESH)
    pl.semaphore_signal(barrier, inc=1, device_id={"blk": k ^ 1}, device_id_type=MESH)

    if G == 4 and C == 4:
        inner, odd = ((d + 1) // 2) % 2, k % 2

        def pick4(a, b, c, e):
            low = a if a == b else a + odd * (b - a)
            high = c if c == e else c + odd * (e - c)
            return low if low is high else low + inner * (high - low)

        def orders(*codes):
            lists = [[divmod(code, 10) for code in one] for one in codes]
            return [(pick4(*(o for o, _ in at)), pick4(*(c for _, c in at))) for at in zip(*lists, strict=True)]

        leave = orders(*LEAVE)
        order = orders(*ARRIVE)
        units = [[(0, c) for c in range(C)], order[:4], order[4:8], order[8:10], order[10:]]
    else:
        leave = [(o, c) for o in range(1, G) for c in range(C)]
        units = [[(o, c) for o in range(G) for c in range(C)]]
    rank = sizes[0]

    def fixed(start, multiple=16):
        return start if isinstance(start, int) else pl.multiple_of(start, multiple)

    def slots(o, c):
        return pl.ds(fixed(o * cap + c * rank), rank)

    def group(o):
        return pl.ds(fixed(o * cap), cap)

    def block(o, c, h=0, many=1):
        return pl.ds(fixed(o * (H * cap) + (c * H + h) * rank), many * rank)

    def span(u):
        return pl.ds(sum(len(v) for v in units[:u]) * rank, len(units[u]) * rank)

    def z_copy(o, c):
        return pltpu.make_async_remote_copy(
            src_ref=outgoing.at[slots(o, c)], dst_ref=rows.at[block(o, c)],
            send_sem=sent.at[0], recv_sem=z_rs.at[c, o - 1],
            device_id={"db": d ^ o}, device_id_type=MESH)

    def x_copy(u, o, c, h, step):
        return pltpu.make_async_remote_copy(
            src_ref=rows.at[block(o, c, h)], dst_ref=rows.at[block(o, c, h + step)],
            send_sem=sent.at[1], recv_sem=x_rs.at[u, h + step - 1],
            device_id={"blk": k ^ (2 * step)}, device_id_type=MESH)

    def s_copy(t):
        return pltpu.make_async_remote_copy(
            src_ref=slab.at[0, t], dst_ref=slab.at[1, t],
            send_sem=sent.at[2], recv_sem=s_rs.at[0],
            device_id={"blk": k ^ 1}, device_id_type=MESH)

    def xb_copy(u, h):
        return pltpu.make_async_remote_copy(
            src_ref=xout.at[h - 1, span(u)], dst_ref=xin.at[h - 1, span(u)],
            send_sem=sent.at[3], recv_sem=xb_rs.at[u, h - 1],
            device_id={"blk": k ^ (2 * h)}, device_id_type=MESH)

    def zb_copy(o, c):
        return pltpu.make_async_remote_copy(
            src_ref=back.at[slots(o, c)], dst_ref=ans.at[slots(o, c)],
            send_sem=sent.at[4], recv_sem=zb_rs.at[o - 1],
            device_id={"db": d ^ o}, device_id_type=MESH)

    def yb_copy(u, i):
        o, c = units[u][i]
        return pltpu.make_async_remote_copy(
            src_ref=xout.at[0, pl.ds((sum(len(v) for v in units[:u]) + i) * rank, rank)],
            dst_ref=ans2.at[slots(o - 1, c)],
            send_sem=sent.at[3], recv_sem=yb_rs.at[0],
            device_id={"db": d ^ o, "blk": k ^ 2}, device_id_type=MESH)

    def await_bytes(ref, sem):
        pltpu.make_async_copy(ref, ref, sem).wait()

    def local(o):
        return isinstance(o, int) and o == 0

    load_r.wait()
    target = routes_ref[...]
    pad = max(8, G)
    hot = jnp.where(lax.broadcasted_iota(jnp.int32, (pad, n), 0) == target, 1.0, 0.0)
    before = jnp.where(
        lax.broadcasted_iota(jnp.int32, (n, n), 0) < lax.broadcasted_iota(jnp.int32, (n, n), 1),
        1.0, 0.0).astype(bf16)
    earlier = jnp.dot(hot.astype(bf16), before, preferred_element_type=f32)
    slot = jnp.sum(hot * earlier, axis=0, keepdims=True).astype(jnp.int32)
    position = (target ^ d) * cap + slot

    def leave_local():
        for c in range(C):
            if H > 1:
                x_copy(0, 0, c, 0, 1).start()

    load_q.wait()
    picks = [
        jnp.where(
            lax.broadcasted_iota(jnp.int32, (cap, n), 0) + o * cap == position, 1.0, 0.0
        ).astype(bf16) for o in range(G)]
    for o in range(G):
        chooser[group(o), :] = picks[o]
    load_p[0].wait()
    projected = jnp.dot(q_ref[:, :half], p_ref[:half], preferred_element_type=f32)
    load_p[1].wait()
    load_v.start()
    projected += jnp.dot(q_ref[:, half:], p_ref[half:], preferred_element_type=f32)
    normed = (
        projected * lax.rsqrt(jnp.sum(projected * projected, axis=1, keepdims=True) + 1e-06)
    ).astype(bf16)
    chosen = jnp.dot(chooser[...], normed, preferred_element_type=f32).astype(bf16)
    outgoing[cap:, :] = chosen[cap:]
    for c in range(C):
        rows[block(0, c)] = chosen[c * rank:(c + 1) * rank]
    pl.semaphore_wait(barrier, G - 1 + H)
    z_copy(*leave[0]).start()
    leave_local()
    for o, c in leave[1:]:
        z_copy(o, c).start()

    def relay(u, i):
        o, c = units[u][i]
        z_copy(o, c).wait_recv()
        if H > 1:
            x_copy(u, o, c, 0, 1).start()

    load_b.wait()
    load_v.wait()
    bins = bins_ref[...]
    inner_mask = jnp.where(
        lax.broadcasted_iota(jnp.int32, (BINS, BINS), 0)
        < lax.broadcasted_iota(jnp.int32, (BINS, BINS), 1), 1.0, 0.0).astype(bf16)
    run = jnp.zeros((BINS, 1), f32)
    places = []
    for s in range(width // BINS):
        mine = bins[:, s * BINS:(s + 1) * BINS]
        hot = jnp.where(lax.broadcasted_iota(jnp.int32, (BINS, BINS), 0) == mine, 1.0, 0.0)
        earlier = jnp.dot(hot.astype(bf16), inner_mask, preferred_element_type=f32) + run
        turn = jnp.sum(hot * earlier, axis=0, keepdims=True).astype(jnp.int32)
        places.append(turn * BINS + mine)
        run = run + jnp.sum(hot, axis=1, keepdims=True)
    place = jnp.concatenate(places, axis=1)
    for t in range(tiles):
        move = jnp.where(
            lax.broadcasted_iota(jnp.int32, (TILE, width), 0) + t * TILE == place, 1.0, 0.0
        ).astype(bf16)
        slab[0, t] = lax.dot_general(
            raw[...], move, (((1,), (1,)), ((), ())), preferred_element_type=f32).astype(bf16)
        s_copy(t).start()

    def whole(u):
        return rows.at[pl.ds(0, len(units[u]) * rank)]

    def spread(u):
        step = 2
        while step < H:
            for h in range(step):
                if h >= step // 2:
                    await_bytes(whole(u), x_rs.at[u, h - 1])
                for o, c in units[u]:
                    x_copy(u, o, c, h, step).start()
            step *= 2

    def score(u, straight=False):
        spread(u)
        for h in range(max(1, H // 2), H):
            await_bytes(whole(u), x_rs.at[u, h - 1])
        if u == 0:
            await_bytes(slab.at[1], s_rs.at[0])
        x = jnp.concatenate([rows[block(o, c, 0, H)] for o, c in units[u]], axis=0)
        best = None
        for side in range(2):
            for t in range(tiles):
                sc = jnp.dot(x, slab[side, t], preferred_element_type=f32)
                top = jnp.maximum(sc[:, :BINS], sc[:, BINS:])
                best = top if best is None else jnp.maximum(best, top)
        best = encode(best).astype(bf16)
        to = sum(len(v) for v in units[:u]) * rank
        for i in range(len(units[u])):
            for h in range(H):
                piece = best[(i * H + h) * rank:(i * H + h + 1) * rank]
                if h == 0:
                    own[pl.ds(to + i * rank, rank)] = piece
                else:
                    xout[h - 1, pl.ds(to + i * rank, rank)] = piece
        if straight and direct:
            for i in range(len(units[u])):
                yb_copy(u, i).start()
        elif len(units) == 1:
            share(u)

    def share(u):
        for h in range(1, H):
            xb_copy(u, h).start()

    def combine(u, straight=False):
        total = own[span(u)]
        for h in range(1, 1 if straight and direct else H):
            xb_copy(u, h).wait_recv()
            total = jnp.maximum(total, xin[h - 1, span(u)])
        for i, (o, c) in enumerate(units[u]):
            piece = total[i * rank:(i + 1) * rank]
            if isinstance(o, int) and o == 0:
                ans[slots(0, c)] = piece
            else:
                back[slots(o, c)] = piece
                zb_copy(o, c).start()

    column = jnp.transpose(jnp.broadcast_to(position.astype(f32), (8, n)))[:, :1].astype(jnp.int32)
    chooser_t[...] = jnp.where(
        lax.broadcasted_iota(jnp.int32, (n, G * cap), 1) == column, 1.0, 0.0).astype(bf16)

    if len(units) > 1:
        def relays(first, last):
            for p in range(first, last):
                if p < 8:
                    relay(1 + p // 4, p % 4)
                else:
                    relay(3 + (p - 8) // 2, p % 2)

        def finish(last=()):
            score(3, True)
            combine(3, True)
            share(0)
            for u in last:
                combine(u)
            score(4, True)
            combine(4, True)
            combine(0)

        @pl.when(inner == 0)
        def _():
            relays(0, 4)
            score(0)
            relays(4, 8)
            score(1)
            share(1)
            relays(8, 11)
            score(2, True)
            combine(2, True)
            relays(11, 12)
            finish((1,))

        @pl.when(inner == 1)
        def _():
            relays(8, 9)
            relays(0, 4)
            score(0)
            relays(4, 7)
            score(1)
            share(1)
            relays(7, 8)
            relays(9, 10)
            combine(1)
            relays(10, 12)
            score(2, True)
            combine(2, True)
            finish()
    else:
        for i, (o, c) in enumerate(units[0]):
            if o:
                relay(0, i)
        score(0)
        combine(0)
    total = jnp.dot(chooser_t[:, :cap], ans[:cap], preferred_element_type=f32)
    for o in range(1, G):
        await_bytes(ans.at[group(o)], zb_rs.at[o - 1])
    if direct:
        counts = [
            sum(code // 10 == o for o, at in ((1, 2 - i + j), (2, 2 - i + j), (3, i + j)) for code in ARRIVE[at][LATE[at]:])
            for i in (0, 2) for j in (0, 1)]
        late = pick4(*counts)
        for some in sorted(set(counts)):
            pl.when(late == some)(lambda some=some: await_bytes(ans2.at[pl.ds(0, some * rank)], yb_rs.at[0]))
    found = ans[cap:]
    if direct:
        found = jnp.maximum(found, ans2[...])
    total = total + jnp.dot(chooser_t[:, cap:], found, preferred_element_type=f32)
    out_ref[...] = total.astype(bf16)

    away = pl.ds(cap, (G - 1) * cap)
    await_bytes(outgoing.at[away], sent.at[0])
    if H > 1:
        await_bytes(rows.at[pl.ds(0, (H - 1) * G * cap)], sent.at[1])
        await_bytes(xout, sent.at[3])
    await_bytes(slab.at[0], sent.at[2])
    await_bytes(back.at[away], sent.at[4])


def per_device(queries, projection, vectors, bins, routes):
    G, NB = lax.axis_size("db"), lax.axis_size("blk")
    n, depth = queries.shape
    width = vectors.shape[1]
    cap = 2 * n // G
    sizes = [cap // 4] * 4 if cap % 64 == 0 else [cap]
    C = len(sizes)
    H = NB // 2
    tiles = width // TILE
    units = 5 if G == 4 and C == 4 else 1
    f32, bf16 = jnp.float32, jnp.bfloat16
    hbm = pl.BlockSpec(memory_space=pltpu.HBM)
    vmem = pl.BlockSpec(memory_space=pltpu.VMEM)
    dma = pltpu.SemaphoreType.DMA
    code = pl.pallas_call(
        functools.partial(kernel, G, NB, cap, tuple(sizes)),
        out_shape=pltpu.VMEM((n, BINS), bf16),
        in_specs=[hbm] * 5,
        out_specs=vmem,
        scratch_shapes=[
            pltpu.VMEM((n, depth), bf16),
            pltpu.VMEM(projection.shape, bf16),
            pltpu.VMEM((depth, width), bf16),
            pltpu.VMEM((1, width), jnp.int32),
            pltpu.VMEM((1, n), jnp.int32),
            pltpu.VMEM((2, tiles, depth, TILE), bf16),
            pltpu.VMEM((G * cap, n), bf16),
            pltpu.VMEM((G * cap, depth), bf16),
            pltpu.VMEM((H * G * cap, depth), bf16),
            pltpu.VMEM((G * cap, BINS), bf16),
            pltpu.VMEM((max(1, H - 1), G * cap, BINS), bf16),
            pltpu.VMEM((max(1, H - 1), G * cap, BINS), bf16),
            pltpu.VMEM((G * cap, BINS), bf16),
            pltpu.VMEM((G * cap, BINS), bf16),
            pltpu.VMEM((max(1, G - 1) * cap, BINS), bf16),
            pltpu.VMEM((n, G * cap), bf16),
            dma((6,)),
            dma((C, G - 1)),
            dma((units, max(1, H - 1))),
            dma((1,)),
            dma((min(units, 2), max(1, H - 1))),
            dma((G - 1,)),
            dma((1,)),
            dma((5,)),
        ],
        compiler_params=pltpu.CompilerParams(
            collective_id=0, has_side_effects=True, vmem_limit_bytes=60 * 1024 * 1024),
    )(queries, projection, vectors, bins.reshape(1, -1), routes.reshape(1, -1))
    return logit_scale * decode(code.astype(f32))


def solution(mesh):
    in_specs = (
        P(("parts", "db", "blk"), None),
        P(),
        P(None, ("parts", "db", "blk")),
        P(("parts", "db", "blk")),
        P(("parts", "db", "blk"), None),
    )
    out_specs = P(("parts", "db", "blk"), None)
    return jax.shard_map(
        per_device, mesh=mesh, in_specs=in_specs, out_specs=out_specs, check_vma=False
    )
```
